32 devices in a mesh: azim: 8 (over z, y), axial: 4 (over x, core).
Axes of the slice: x: 2, y: 2, z: 4, core: 2. Of those that a mesh axis runs over, the one named last changes fastest.
Arguments:
- observed_heights: bfloat16 [4, 8, 1024, 1024], P('axial', 'azim'), may hold values from -6 to 6
- ref_map: float32 [1024, 1024], P(('azim', 'axial')), may hold values from -3 to 3
- coefs: float32 [4, 8, 4], P('axial', 'azim'), may hold values from -1.8 to 1.8
- shifts: float32 [4, 8], P('axial', 'azim'), may hold values from 0.1 to 0.9
- pair_offset: int32 [4, 8, 16], P('axial', 'azim'), may hold values from 0 to 255
- pair_width: int32 [4, 8, 16], P('axial', 'azim'), may hold values from 128 to 512
Outputs:
- refined_map: float32 [1024, 1024], P(('azim', 'axial'))
- refined_coefs: float32 [4, 8, 4], P('axial', 'azim')
The draws below stay inside these ranges and needn't reach their ends.
All inputs are finite; a program needn't handle non-finite values.
Results may differ from the reference program's by a relative error of at most 0.0041.
Values may be sent and summed in bfloat16 or wider, within the bound.
No kernel may reach another device: no remote copies, remote signals or barrier semaphores. Data moves between devices by JAX's collectives and lax.ppermute only.
A program may use at most 64 MiB of HBM per device.

```python
import math
import jax
import jax.numpy as jnp
from jax import lax

ANGULAR_SAMPLES = 1024
LENGTH_SAMPLES = 1024
HALF = 512
KTERMS = 4
PAIRS_SUB = 16
PASSES = 2
LENGTHWISE_TILES = 4
CIRCUM_TILES = 8
TILE_AMOUNT = 32


def touch_ends(result, own_key, least, high):
    longest = result.shape.index(max(result.shape))
    spots = []
    for shift in (0, 1):
        where = [jax.random.randint(jax.random.fold_in(own_key, axis), (), 0, length) for axis, length in enumerate(result.shape)]
        where[longest] = (where[longest] + shift) % result.shape[longest]
        spots.append(tuple(where))
    return result.at[spots[0]].set(least).at[spots[1]].set(high)


def levels(key, shape, shards, least, largest):
    factor_of, own = 1.0, jax.random.fold_in(key, 6)
    for dim, shards_of in shards:
        heights = jnp.exp(jax.random.uniform(jax.random.fold_in(own, dim), (shards_of,), jnp.float32, least / len(shards), largest / len(shards)))
        factor_of = factor_of * jnp.repeat(heights, shape[dim] // shards_of).reshape([-1 if axis == dim else 1 for axis in range(len(shape))])
    return factor_of


def centred(stream_key, dims, scale, limit, split=(), kind=jnp.bfloat16):
    loudness = levels(stream_key, dims, split, -0.22, 0.18) if split else 1.0
    result = jax.random.normal(stream_key, dims, jnp.float32) * scale * loudness
    return jnp.minimum(jnp.maximum(result, -limit), limit).astype(kind)


def setup_inputs(seed: int = 0) -> dict:
    splits = jax.random.split(jax.random.key(seed), 7)
    return {
        "observed_heights": centred(splits[0], (LENGTHWISE_TILES, CIRCUM_TILES, LENGTH_SAMPLES, ANGULAR_SAMPLES), 1.0, 6.0, ((0, 4), (1, 8))),
        "ref_map": centred(splits[1], (LENGTH_SAMPLES, ANGULAR_SAMPLES), 0.5, 3.0, ((0, 32),), jnp.float32),
        "coefs": centred(splits[2], (LENGTHWISE_TILES, CIRCUM_TILES, KTERMS), 0.3, 1.8, ((0, 4), (1, 8)), jnp.float32),
        "shifts": jnp.clip(0.1 + 0.79999997 * jax.random.uniform(splits[3], (LENGTHWISE_TILES, CIRCUM_TILES), jnp.float32) ** levels(splits[3], (LENGTHWISE_TILES, CIRCUM_TILES), ((0, 4), (1, 8)), -0.2, 0.2), 0.1, 0.9),
        "pair_offset": touch_ends(jax.random.randint(splits[4], (LENGTHWISE_TILES, CIRCUM_TILES, PAIRS_SUB), 0, HALF // 2), jax.random.fold_in(splits[4], 1), 0, (HALF // 2) - 1).astype(jnp.int32),
        "pair_width": touch_ends(jax.random.randint(splits[5], (LENGTHWISE_TILES, CIRCUM_TILES, PAIRS_SUB), HALF // 4, HALF + 1), jax.random.fold_in(splits[5], 1), HALF // 4, HALF).astype(jnp.int32),
    }


window_width = 16.0

def grid_terms(row_total, col_total):
    lengthwise = (jnp.arange(row_total, dtype=jnp.float32) - 0.5 * (row_total - 1)) * (2.0 / row_total)
    angular_place = (jnp.arange(col_total, dtype=jnp.float32) - 0.5 * (col_total - 1)) * (2.0 / col_total)
    return (lengthwise[:, None], angular_place[None, :])

def registration(coef_vec, lengthwise, angular_place):
    return coef_vec[0] + coef_vec[1] * angular_place + coef_vec[2] * lengthwise + coef_vec[3] * (angular_place * angular_place + lengthwise * lengthwise - 2.0 / 3.0)

def resampler(shift_value, col_total):
    source = jnp.arange(col_total, dtype=jnp.float32)[:, None]
    target = jnp.arange(col_total, dtype=jnp.float32)[None, :]
    offset = source - target - shift_value
    return (jnp.sinc(offset) * jnp.exp(-(offset * offset) / (window_width * window_width))).astype(jnp.bfloat16)

def coef_gradient(pulled, lengthwise, angular_place):
    return jnp.stack([jnp.sum(pulled), jnp.sum(pulled * angular_place), jnp.sum(pulled * lengthwise), jnp.sum(pulled * (angular_place * angular_place + lengthwise * lengthwise - 2.0 / 3.0))])

def reference(observed_heights, ref_map, coefs, shifts, pair_offset, pair_width):
    half_cols = ANGULAR_SAMPLES // 2
    band_rows = LENGTH_SAMPLES // PAIRS_SUB
    lengthwise, angular_place = grid_terms(LENGTH_SAMPLES, ANGULAR_SAMPLES)
    columns = jnp.arange(half_cols, dtype=jnp.int32)
    lower = pair_offset[..., None]
    window_mask = (columns >= lower) & (columns < lower + pair_width[..., None])
    unrolled_heights = observed_heights.reshape(TILE_AMOUNT, LENGTH_SAMPLES, ANGULAR_SAMPLES)
    unrolled_offset_terms = shifts.reshape(TILE_AMOUNT)
    unrolled_factors = coefs.reshape(TILE_AMOUNT, KTERMS)
    for pass_index in range(PASSES):
        datum_error_start = ref_map.astype(jnp.bfloat16)

        def predictive_pass(tile_index):
            height_map_solo, factor_vector_solo, displacement_solo = tile_index
            repaired_heights = (height_map_solo.astype(jnp.float32) - datum_error_start.astype(jnp.float32) - registration(factor_vector_solo, lengthwise, angular_place)).astype(jnp.bfloat16)
            return jnp.dot(repaired_heights, resampler(displacement_solo, ANGULAR_SAMPLES), preferred_element_type=jnp.float32).astype(jnp.bfloat16)
        regridded = lax.map(predictive_pass, (unrolled_heights, unrolled_factors, unrolled_offset_terms)).reshape(LENGTHWISE_TILES, CIRCUM_TILES, LENGTH_SAMPLES, ANGULAR_SAMPLES)
        right_part = regridded[..., half_cols:].astype(jnp.float32)
        left_next = jnp.roll(regridded[..., :half_cols], -1, axis=1).astype(jnp.float32)
        difference = (right_part - left_next).reshape(LENGTHWISE_TILES, CIRCUM_TILES, PAIRS_SUB, band_rows, half_cols)
        seam_rows = jnp.where(window_mask[:, :, :, None, :], difference, 0.0).astype(jnp.bfloat16)
        seam_rows = seam_rows.reshape(LENGTHWISE_TILES, CIRCUM_TILES, LENGTH_SAMPLES, half_cols)
        upstream = jnp.concatenate([-jnp.roll(seam_rows, 1, axis=1), seam_rows], axis=3).reshape(TILE_AMOUNT, LENGTH_SAMPLES, ANGULAR_SAMPLES)

        def backward(total, tile_index):
            up_one, displacement_solo = tile_index
            pulled = lax.dot_general(up_one, resampler(displacement_solo, ANGULAR_SAMPLES), (((1,), (1,)), ((), ())), preferred_element_type=jnp.float32)
            return (total + pulled, coef_gradient(pulled, lengthwise, angular_place))
        total, coef_grads = lax.scan(backward, jnp.zeros((LENGTH_SAMPLES, ANGULAR_SAMPLES), jnp.float32), (upstream, unrolled_offset_terms))
        ref_map = ref_map + total / math.sqrt(TILE_AMOUNT)
        unrolled_factors = unrolled_factors + coef_grads / (LENGTH_SAMPLES * ANGULAR_SAMPLES)
    return (ref_map, unrolled_factors.reshape(LENGTHWISE_TILES, CIRCUM_TILES, KTERMS))
```

```python
import functools
import math

import jax
import jax.numpy as jnp
from jax import lax
from jax.experimental import pallas as pl
from jax.experimental.pallas import tpu as pltpu
from jax.sharding import PartitionSpec as P

PASSES = 2
AXES = ("azim", "axial")
WINDOW = 16.0
LANE = 128
WIDE = 256
REACH = 2
SPAN = 512


def tap_tables(shifts):
    place = jnp.arange(2 * SPAN, dtype=jnp.float32) - SPAN
    lag = jnp.stack([-place, place])[None]
    offset = lag - shifts[:, None, None]
    return jnp.sinc(offset) * jnp.exp(-(offset * offset) / (WINDOW * WINDOW))


def butterfly_sum(value):
    for axis in ("axial", "azim"):
        size = lax.axis_size(axis)
        step = 1
        while step < size:
            value = value + lax.ppermute(value, axis, [(i, i ^ step) for i in range(size)])
            step *= 2
    return value


def build_bands(tap_ref, band_ref, tiles):
    def one(s, carry):
        for way in range(2):
            taps = jnp.broadcast_to(tap_ref[s, way : way + 1, :], (LANE, 2 * SPAN))
            skewed = pltpu.roll(taps, 0, 1, stride=1, stride_axis=0)
            first = SPAN - REACH * LANE
            band_ref[s, way] = skewed[:, first : first + (2 * REACH + 1) * LANE].astype(jnp.bfloat16)
        return carry

    lax.fori_loop(0, tiles, one, 0)


def wide_matrix(band_ref, s, way):
    def block(distance):
        if abs(distance) > REACH:
            return jnp.zeros((LANE, LANE), jnp.bfloat16)
        start = (REACH - distance) * LANE
        return band_ref[s, way, :, start : start + LANE]

    rows = []
    for row in range(-2, 4):
        rows.append(jnp.concatenate([block(row - col) for col in range(2)], axis=1))
    return jnp.concatenate(rows, axis=0)


def spread(stacked, rows):
    if rows % 16:
        stacked = stacked.astype(jnp.float32)
    edge = jnp.zeros((rows, WIDE), stacked.dtype)
    before = jnp.concatenate([edge, stacked[:-rows]], axis=0)
    after = jnp.concatenate([stacked[rows:], edge], axis=0)
    return jnp.concatenate([before, stacked, after], axis=1).astype(jnp.bfloat16)


def stack_blocks(value):
    return jnp.concatenate(
        [value[:, k : k + WIDE] for k in range(0, value.shape[1], WIDE)], axis=0
    )


def pass_kernel(
    tiles, neighbour, scale, height_ref, ref_ref, tap_ref, col_ref, row_ref, coef_ref, low_ref, high_ref,
    map_ref, grad_ref, band_ref, resampled_ref, total_ref, ref_low_ref
):
    rows, cols = ref_ref.shape
    build_bands(tap_ref, band_ref, tiles)
    ref_low_ref[...] = ref_ref[...].astype(jnp.bfloat16).astype(jnp.float32)

    def forward(s, carry):
        az = col_ref[0:1, :]
        ax = row_ref[:, 0:1]
        shape = (
            coef_ref[4 * s]
            + coef_ref[4 * s + 1] * az
            + coef_ref[4 * s + 2] * ax
            + coef_ref[4 * s + 3] * (az * az + ax * ax - 2.0 / 3.0)
        )
        corrected = height_ref[s].astype(jnp.float32) - ref_low_ref[...] - shape
        stacked = stack_blocks(corrected).astype(jnp.bfloat16)
        out = jnp.dot(
            spread(stacked, rows), wide_matrix(band_ref, s, 0), preferred_element_type=jnp.float32
        )
        resampled_ref[s] = out.astype(jnp.bfloat16)
        return carry

    lax.fori_loop(0, tiles, forward, 0)
    total_ref[...] = jnp.zeros_like(total_ref)
    column = lax.broadcasted_iota(jnp.int32, (2 * rows, WIDE), 1) + jnp.where(
        lax.broadcasted_iota(jnp.int32, (2 * rows, WIDE), 0) >= rows, WIDE, 0
    )

    def seam(left, right):
        difference = resampled_ref[left, 2 * rows :, :].astype(jnp.float32) - resampled_ref[
            right, : 2 * rows, :
        ].astype(jnp.float32)
        inside = (column >= low_ref[left]) & (column < high_ref[left])
        return jnp.where(inside, difference, 0.0)

    def backward(s, carry):
        before = jnp.where(s >= neighbour, s - neighbour, s - neighbour + tiles)
        after = jnp.where(s + neighbour < tiles, s + neighbour, s + neighbour - tiles)
        upstream = jnp.concatenate([-seam(before, s), seam(s, after)], axis=0).astype(jnp.bfloat16)
        pulled = jnp.dot(
            spread(upstream, rows), wide_matrix(band_ref, s, 1), preferred_element_type=jnp.float32
        )
        total_ref[...] += pulled
        ax = row_ref[:, :]
        plain, tilted, bent = [], [], []
        for k in range(cols // WIDE):
            block = pulled[k * rows : (k + 1) * rows].reshape(rows // 8, 8, WIDE)
            weight = jnp.concatenate([ax, ax], axis=1).reshape(rows // 8, 8, WIDE)
            first = block * weight
            plain.append(jnp.sum(block, axis=0))
            tilted.append(jnp.sum(first, axis=0))
            bent.append(jnp.sum(first * weight, axis=0))
        plain = jnp.concatenate(plain, axis=1)
        tilted = jnp.concatenate(tilted, axis=1)
        bent = jnp.concatenate(bent, axis=1)
        az = col_ref[0:1, :]
        leaning = plain * az
        sums = [plain, leaning, tilted, leaning * az + bent - plain * (2.0 / 3.0)]
        folded = [
            sum(value[:, k : k + LANE] for k in range(0, cols, LANE)) for value in sums
        ]
        grad_ref[s] = jnp.concatenate([jnp.sum(v, axis=0, keepdims=True) for v in folded], axis=0)
        return carry

    lax.fori_loop(0, tiles, backward, 0)
    for k in range(cols // WIDE):
        part = slice(k * WIDE, (k + 1) * WIDE)
        map_ref[:, part] = ref_ref[:, part] + total_ref[k * rows : (k + 1) * rows, :] / scale


def one_pass(heights, ref_rows, taps, col_terms, row_terms, coefs, low, high, neighbour):
    tiles, rows, cols = heights.shape
    vmem = pl.BlockSpec(memory_space=pltpu.VMEM)
    smem = pl.BlockSpec(memory_space=pltpu.SMEM)
    body = functools.partial(pass_kernel, tiles, neighbour, math.sqrt(tiles))
    return pl.pallas_call(
        body,
        out_shape=(
            jax.ShapeDtypeStruct((rows, cols), jnp.float32),
            jax.ShapeDtypeStruct((tiles, 4, LANE), jnp.float32),
        ),
        in_specs=[vmem] * 5 + [smem] * 3,
        out_specs=(vmem, vmem),
        scratch_shapes=[
            pltpu.VMEM((tiles, 2, LANE, (2 * REACH + 1) * LANE), jnp.bfloat16),
            pltpu.VMEM((tiles, 4 * rows, WIDE), jnp.bfloat16),
            pltpu.VMEM((4 * rows, WIDE), jnp.float32),
            pltpu.VMEM((rows, cols), jnp.float32),
        ],
        compiler_params=pltpu.CompilerParams(vmem_limit_bytes=56 * 1024 * 1024),
    )(heights, ref_rows, taps, col_terms, row_terms, coefs.reshape(-1), low, high)


def local(observed_heights, ref_map, coefs, shifts, pair_offset, pair_width):
    rows, cols = ref_map.shape
    axial_size = lax.axis_size("axial")
    tiles = lax.axis_size("azim") * axial_size
    me = lax.axis_index(AXES)
    row_total = observed_heights.shape[2]
    pair_count = pair_offset.shape[2]
    pair = me * rows // (row_total // pair_count)

    words = jnp.concatenate(
        [
            coefs[0, 0],
            shifts[0],
            pair_offset[0, 0].astype(jnp.float32),
            pair_width[0, 0].astype(jnp.float32),
        ]
    )
    words = jnp.pad(words, (0, LANE - words.shape[0]))[None]
    table = lax.all_gather(words, AXES, axis=0, tiled=True)
    heights = lax.all_to_all(
        observed_heights[0, 0].reshape(tiles, rows, cols), AXES, 0, 0, tiled=True
    )
    coef_now = table[:, :4]
    taps = tap_tables(table[:, 4])
    low = lax.dynamic_index_in_dim(table, 5 + pair, 1, keepdims=False).astype(jnp.int32)
    width = lax.dynamic_index_in_dim(table, 5 + pair_count + pair, 1, keepdims=False)
    high = low + width.astype(jnp.int32)

    row_place = (me * rows).astype(jnp.float32) + jnp.arange(rows, dtype=jnp.float32)
    row_terms = (row_place - 0.5 * (row_total - 1)) * (2.0 / row_total)
    row_terms = jnp.broadcast_to(row_terms[:, None], (rows, LANE))
    col_terms = (jnp.arange(cols, dtype=jnp.float32) - 0.5 * (cols - 1)) * (2.0 / cols)
    col_terms = jnp.broadcast_to(col_terms[None], (8, cols))

    ref_rows = ref_map
    for _ in range(PASSES):
        ref_rows, partial = one_pass(
            heights, ref_rows, taps, col_terms, row_terms, coef_now, low, high, axial_size
        )
        grads = butterfly_sum(jnp.sum(partial, axis=2))
        coef_now = coef_now + grads / (row_total * cols)
    mine = lax.dynamic_slice_in_dim(coef_now, me, 1, axis=0)
    return (ref_rows, mine[None])


def solution(mesh):
    in_specs = (
        P("axial", "azim", None, None),
        P(("azim", "axial"), None),
        P("axial", "azim", None),
        P("axial", "azim"),
        P("axial", "azim", None),
        P("axial", "azim", None),
    )
    out_specs = (P(("azim", "axial"), None), P("axial", "azim", None))
    return jax.shard_map(local, mesh=mesh, in_specs=in_specs, out_specs=out_specs, check_vma=False)
```

```python
import functools
import math

import jax
import jax.numpy as jnp
from jax import lax
from jax.experimental import pallas as pl
from jax.experimental.pallas import tpu as pltpu
from jax.sharding import PartitionSpec as P

AXES = ("azim", "axial")
WINDOW = 16.0
LANE = 128
WIDE = 256
REACH = 2
BAND = (2 * REACH + 1) * LANE
SPAN = 512
GROUP = 4
HALF_LANE = 64
VMEM_MAIN = 56 * 1024 * 1024
EXACT = lax.Precision.HIGHEST


def exchange(value, axis, steps):
    size = lax.axis_size(axis)
    return sum(lax.ppermute(value, axis, [(i, i ^ k) for i in range(size)]) for k in steps)


def gather_rows(value):
    azim, axial = lax.axis_size("azim"), lax.axis_size("axial")
    value = value + exchange(value, "azim", range(2, azim, 2))
    value = value + exchange(value, "azim", [1])
    step = axial // 2
    while step:
        value = value + exchange(value, "axial", [step])
        step //= 2
    return value


def tap_values(offset):
    centre = offset == 0.0
    angle = jnp.where(centre, 1.0, math.pi * offset)
    sinc = jnp.where(centre, 1.0, jnp.sin(angle) / angle)
    return sinc * jnp.exp(-(offset * offset) / (WINDOW * WINDOW))


def wide_matrix(band_ref, s, way):
    def block(distance):
        if abs(distance) > REACH:
            return jnp.zeros((LANE, LANE), jnp.bfloat16)
        start = (REACH - distance) * LANE
        return band_ref[s, way, :, start : start + LANE]

    rows = []
    for row in range(-2, 4):
        rows.append(jnp.concatenate([block(row - col) for col in range(2)], axis=1))
    return jnp.concatenate(rows, axis=0)


def spread(stacked, rows):
    if rows % 16:
        stacked = stacked.astype(jnp.float32)
    edge = jnp.zeros((rows, WIDE), stacked.dtype)
    before = jnp.concatenate([edge, stacked[:-rows]], axis=0)
    after = jnp.concatenate([stacked[rows:], edge], axis=0)
    return jnp.concatenate([before, stacked, after], axis=1).astype(jnp.bfloat16)


def stack_blocks(value):
    return jnp.concatenate(
        [value[:, k : k + WIDE] for k in range(0, value.shape[1], WIDE)], axis=0
    )


def mixed(stacked, rows, band_ref, s, way):
    return jnp.dot(
        spread(stacked, rows), wide_matrix(band_ref, s, way), preferred_element_type=jnp.float32
    )


def neighbours(s, tiles, stride):
    before = jnp.where(s >= stride, s - stride, s - stride + tiles)
    after = jnp.where(s + stride < tiles, s + stride, s + stride - tiles)
    return before, after


def two_parts(value):
    high = value.astype(jnp.bfloat16).astype(jnp.float32)
    return high, value - high


def prepare_kernel(
    tiles, stride, pair_count, pair_ref, words_ref, table_ref, col_ref,
    band_ref, effect_ref, moment_ref, tap_ref, seen_ref, base_ref
):
    cols = col_ref.shape[1]
    blocks = cols // WIDE
    pair = pair_ref[0]
    place = lax.broadcasted_iota(jnp.int32, (tiles, 2 * SPAN), 1).astype(jnp.float32) - SPAN
    shift = table_ref[:, 4:5]
    tap_ref[0] = tap_values(-place - shift)
    tap_ref[1] = tap_values(place - shift)
    az = col_ref[0:1, :]
    row = lax.broadcasted_iota(jnp.int32, (8, cols), 0)
    base = jnp.where(row == 0, 1.0, jnp.where(row == 1, az, jnp.where(row == 2, az * az, 0.0)))
    high, low = two_parts(base)
    base = jnp.concatenate([high, low], axis=0)
    base_ref[...] = spread(stack_blocks(base).astype(jnp.bfloat16), 16)
    effect_ref[...] = jnp.zeros_like(effect_ref)

    def build(s, carry):
        for way in range(2):
            taps = jnp.broadcast_to(tap_ref[way, pl.ds(s, 1), :], (LANE, 2 * SPAN))
            skewed = pltpu.roll(taps, 0, 1, stride=1, stride_axis=0)
            first = SPAN - REACH * LANE
            band_ref[s, way] = skewed[:, first : first + BAND].astype(jnp.bfloat16)
        out = jnp.dot(
            base_ref[...], wide_matrix(band_ref, s, 0), preferred_element_type=jnp.float32
        )
        seen_ref[s] = jnp.sum(out.reshape(blocks, 2, 8, WIDE), axis=1)
        return carry

    lax.fori_loop(0, tiles, build, 0)
    column = lax.broadcasted_iota(jnp.int32, (2, 8, WIDE), 2) + WIDE * lax.broadcasted_iota(
        jnp.int32, (2, 8, WIDE), 0
    )
    column = column.astype(jnp.float32)
    lanes = lax.broadcasted_iota(jnp.int32, (8, LANE), 1)
    az_blocks = [az[:, k : k + LANE] for k in range(0, cols, LANE)]

    def inside(s):
        start = words_ref[s, 5 + pair]
        return (column >= start) & (column < start + words_ref[s, 5 + pair_count + pair])

    def respond(s, carry):
        before, after = neighbours(s, tiles, stride)
        mask_before, mask_own = inside(before), inside(s)
        half = blocks // 2
        own = seen_ref[s]
        zero = jnp.zeros((half, 8, WIDE), jnp.float32)
        parts = [
            jnp.concatenate(
                [jnp.where(mask_before, own[:half], 0.0), jnp.where(mask_own, own[half:], 0.0)], axis=0
            ),
            jnp.concatenate([jnp.where(mask_before, -seen_ref[before][half:], 0.0), zero], axis=0),
            jnp.concatenate([zero, jnp.where(mask_own, -seen_ref[after][:half], 0.0)], axis=0),
        ]
        rows = []
        for block in range(blocks):
            for part in parts:
                rows.extend(two_parts(part[block]))
        out = mixed(jnp.concatenate(rows, axis=0).astype(jnp.bfloat16), 48, band_ref, s, 1)
        out = jnp.sum(out.reshape(blocks, 3, 2, 8, WIDE), axis=2)
        for source, target in enumerate((s, before, after)):
            effect_ref[target] += out[:, source]
            flat = [out[k // 2, source][:, (k % 2) * LANE : (k % 2 + 1) * LANE] for k in range(2 * blocks)]
            first = [f * a for f, a in zip(flat, az_blocks)]
            second = [f * a for f, a in zip(first, az_blocks)]
            sums = [jnp.sum(sum(v), axis=1, keepdims=True) for v in (flat, first, second)]
            moment_ref[s, source] = jnp.where(
                lanes == 0, sums[0], jnp.where(lanes == 1, sums[1], jnp.where(lanes == 2, sums[2], 0.0))
            )
        return carry

    lax.fori_loop(0, tiles, respond, 0)


def prepare(pair, table, col_terms, stride, pair_count):
    tiles = table.shape[0]
    cols = col_terms.shape[1]
    blocks = cols // WIDE
    vmem = pl.BlockSpec(memory_space=pltpu.VMEM)
    smem = pl.BlockSpec(memory_space=pltpu.SMEM)
    return pl.pallas_call(
        functools.partial(prepare_kernel, tiles, stride, pair_count),
        out_shape=(
            jax.ShapeDtypeStruct((tiles, 2, LANE, BAND), jnp.bfloat16),
            jax.ShapeDtypeStruct((tiles, blocks, 8, WIDE), jnp.float32),
            jax.ShapeDtypeStruct((tiles, 3, 8, LANE), jnp.float32),
        ),
        in_specs=[smem, smem, vmem, vmem],
        out_specs=(vmem, vmem, vmem),
        scratch_shapes=[
            pltpu.VMEM((2, tiles, 2 * SPAN), jnp.float32),
            pltpu.VMEM((tiles, blocks, 8, WIDE), jnp.float32),
            pltpu.VMEM((16 * blocks, 3 * WIDE), jnp.bfloat16),
        ],
        compiler_params=pltpu.CompilerParams(vmem_limit_bytes=VMEM_MAIN),
    )(pair, table, table, col_terms)


def passes_kernel(
    tiles, stride, pair_count, scale, pair_ref, words_ref, height_hbm, band_hbm, ref_ref, col_ref, row_ref, extra_ref,
    map_ref, message_ref, height_ref, band_ref, resampled_ref, total_ref, ref_low_ref, sums_ref, sems
):
    rows, cols = ref_ref.shape
    blocks = cols // WIDE
    groups = tiles // GROUP
    pair = pair_ref[0]

    def copies(g):
        part = pl.ds(g * GROUP, GROUP)
        return (
            pltpu.make_async_copy(height_hbm.at[part], height_ref.at[part], sems.at[0, g]),
            pltpu.make_async_copy(band_hbm.at[part], band_ref.at[part], sems.at[1, g]),
        )

    for g in range(groups):
        for copy in copies(g):
            copy.start()

    az = col_ref[0:1, :]
    column = lax.broadcasted_iota(jnp.int32, (2 * rows, WIDE), 1) + jnp.where(
        lax.broadcasted_iota(jnp.int32, (2 * rows, WIDE), 0) >= rows, WIDE, 0
    )
    column = column.astype(jnp.float32)

    def forward(s):
        ax = row_ref[:, 0:1]
        shape = (
            words_ref[s, 0]
            + words_ref[s, 1] * az
            + words_ref[s, 2] * ax
            + words_ref[s, 3] * (az * az + ax * ax - 2.0 / 3.0)
        )
        corrected = height_ref[s].astype(jnp.float32) - ref_low_ref[...] - shape
        out = mixed(stack_blocks(corrected).astype(jnp.bfloat16), rows, band_ref, s, 0)
        resampled_ref[s] = out.astype(jnp.bfloat16)

    def seam(left, right):
        difference = resampled_ref[left, 2 * rows :, :].astype(jnp.float32) - resampled_ref[
            right, : 2 * rows, :
        ].astype(jnp.float32)
        start = words_ref[left, 5 + pair]
        inside = (column >= start) & (column < start + words_ref[left, 5 + pair_count + pair])
        return jnp.where(inside, difference, 0.0)

    def backward(s):
        before, after = neighbours(s, tiles, stride)
        upstream = jnp.concatenate([-seam(before, s), seam(s, after)], axis=0).astype(jnp.bfloat16)
        pulled = mixed(upstream, rows, band_ref, s, 1)
        total_ref[...] += pulled
        plain, tilted, bent = [], [], []
        weight = row_ref[...]
        weight = jnp.concatenate([weight, weight], axis=1).reshape(rows // 8, 8, WIDE)
        for k in range(blocks):
            block = pulled[k * rows : (k + 1) * rows].reshape(rows // 8, 8, WIDE)
            first = block * weight
            plain.append(jnp.sum(block, axis=0))
            tilted.append(jnp.sum(first, axis=0))
            bent.append(jnp.sum(first * weight, axis=0))
        plain = jnp.concatenate(plain, axis=1)
        tilted = jnp.concatenate(tilted, axis=1)
        bent = jnp.concatenate(bent, axis=1)
        leaning = plain * az
        sums = [plain, leaning, tilted, leaning * az + bent - plain * (2.0 / 3.0)]
        folded = [sum(v[:, k : k + LANE] for k in range(0, cols, LANE)) for v in sums]
        return [jnp.sum(v, axis=0, keepdims=True) for v in folded]

    def add_map(source_ref):
        for k in range(blocks):
            part = slice(k * WIDE, (k + 1) * WIDE)
            map_ref[:, part] = source_ref[:, part] + total_ref[k * rows : (k + 1) * rows, :] / scale

    def first_forward(g, carry):
        for copy in copies(g):
            copy.wait()
        for k in range(GROUP):
            forward(g * GROUP + k)
        return carry

    def first_backward(g, carry):
        for k in range(GROUP):
            s = g * GROUP + k
            for term, value in enumerate(backward(s)):
                sums_ref[term, pl.ds(s, 1), :] = value
        return carry

    ref_low_ref[...] = ref_ref[...].astype(jnp.bfloat16).astype(jnp.float32)
    lax.fori_loop(0, groups, first_forward, 0)
    total_ref[...] = jnp.zeros_like(total_ref)
    lax.fori_loop(0, groups, first_backward, 0)
    add_map(ref_ref)

    ones = jnp.ones((8, LANE), jnp.float32)
    turned = []
    for term in range(4):
        line = lax.dot_general(
            ones, sums_ref[term], (((1,), (1,)), ((), ())),
            precision=EXACT, preferred_element_type=jnp.float32,
        )[0:1]
        if tiles < LANE:
            line = jnp.concatenate([line, jnp.zeros((1, LANE - tiles), jnp.float32)], axis=1)
        turned.append(line)
    turned = jnp.concatenate(turned, axis=0)
    low_lanes = lax.broadcasted_iota(jnp.int32, (4, LANE), 1) < HALF_LANE

    def second_forward(g, carry):
        for k in range(GROUP):
            forward(g * GROUP + k)
        return carry

    def second_backward(g, carry):
        for k in range(GROUP):
            s = g * GROUP + k
            value = jnp.concatenate(backward(s), axis=0)
            value = value + pltpu.roll(value, HALF_LANE, 1)
            value = jnp.where(low_lanes, value, extra_ref[s])
            message_ref[s] = jnp.concatenate([turned, value], axis=0)
        return carry

    ref_low_ref[...] = map_ref[...].astype(jnp.bfloat16).astype(jnp.float32)
    lax.fori_loop(0, groups, second_forward, 0)
    total_ref[...] = jnp.zeros_like(total_ref)
    lax.fori_loop(0, groups, second_backward, 0)
    add_map(map_ref)


def passes(pair, table, heights, bands, ref_rows, col_terms, row_terms, extra, stride, pair_count):
    tiles, rows, cols = heights.shape
    vmem = pl.BlockSpec(memory_space=pltpu.VMEM)
    smem = pl.BlockSpec(memory_space=pltpu.SMEM)
    anywhere = pl.BlockSpec(memory_space=pl.ANY)
    return pl.pallas_call(
        functools.partial(passes_kernel, tiles, stride, pair_count, math.sqrt(tiles)),
        out_shape=(
            jax.ShapeDtypeStruct((rows, cols), jnp.float32),
            jax.ShapeDtypeStruct((tiles, 8, LANE), jnp.float32),
        ),
        in_specs=[smem, smem, anywhere, anywhere, vmem, vmem, vmem, vmem],
        out_specs=(vmem, vmem),
        scratch_shapes=[
            pltpu.VMEM((tiles, rows, cols), jnp.bfloat16),
            pltpu.VMEM((tiles, 2, LANE, BAND), jnp.bfloat16),
            pltpu.VMEM((tiles, 4 * rows, WIDE), jnp.bfloat16),
            pltpu.VMEM((4 * rows, WIDE), jnp.float32),
            pltpu.VMEM((rows, cols), jnp.float32),
            pltpu.VMEM((4, tiles, LANE), jnp.float32),
            pltpu.SemaphoreType.DMA((2, tiles // GROUP)),
        ],
        compiler_params=pltpu.CompilerParams(vmem_limit_bytes=VMEM_MAIN),
    )(pair, table, heights, bands, ref_rows, col_terms, row_terms, extra)


def finish_kernel(
    tiles, stride, scale, pixels, me_ref, got_ref, map_ref, effect_ref, row_ref, coef_ref, out_map_ref, out_coef_ref
):
    total = jnp.sum(got_ref[...], axis=0)
    step = total[0:4] / pixels
    later = total[4:8]
    lines = lax.broadcasted_iota(jnp.int32, (8, LANE), 0)
    wide = [jnp.broadcast_to(step[k : k + 1], (8, LANE))[:, :tiles] for k in range(4)]
    lines = lines[:, :tiles]
    flat = jnp.where(
        lines == 0, wide[0] - wide[3] * (2.0 / 3.0),
        jnp.where(lines == 1, wide[2], jnp.where(lines == 2, wide[3], 0.0)),
    )
    only = lines == 0

    def weigh(weights, term):
        return jnp.dot(weights, effect_ref[term], precision=EXACT, preferred_element_type=jnp.float32)

    level = weigh(flat, 0)
    level = level + weigh(jnp.where(only, wide[1], 0.0), 1) + weigh(jnp.where(only, wide[3], 0.0), 2)
    ax = row_ref[:, 0:1]
    change = level[0:1] + ax * (level[1:2] + ax * level[2:3])
    out_map_ref[...] = map_ref[...] - change / scale

    me = me_ref[0]
    before, after = neighbours(me, tiles, stride)
    lane = lax.broadcasted_iota(jnp.int32, (4, LANE), 1)
    reach = jnp.zeros((4, 1), jnp.float32)
    own = None
    for source, target in enumerate((me, before, after)):
        at = jnp.sum(jnp.where(lane == target, step, 0.0), axis=1, keepdims=True)
        own = at if source == 0 else own
        for k in range(4):
            place = HALF_LANE + 4 * source + k
            reach = reach + at[k : k + 1] * later[:, place : place + 1]
    fresh = jnp.sum(jnp.where(lane < HALF_LANE, later, 0.0), axis=1, keepdims=True)
    gain = own + (fresh - reach) / pixels
    line = lax.broadcasted_iota(jnp.int32, (4, LANE), 0)
    gain = jnp.sum(jnp.where(line == lane, gain, 0.0), axis=0, keepdims=True)
    out_coef_ref[...] = coef_ref[...] + gain[:, :4]


def finish(me, got, map_rows, effects, row_terms, coefs, stride, pixels):
    tiles = got.shape[0]
    vmem = pl.BlockSpec(memory_space=pltpu.VMEM)
    smem = pl.BlockSpec(memory_space=pltpu.SMEM)
    return pl.pallas_call(
        functools.partial(finish_kernel, tiles, stride, math.sqrt(tiles), pixels),
        out_shape=(
            jax.ShapeDtypeStruct(map_rows.shape, jnp.float32),
            jax.ShapeDtypeStruct(coefs.shape, jnp.float32),
        ),
        in_specs=[smem] + [vmem] * 5,
        out_specs=(vmem, vmem),
    )(me, got, map_rows, effects, row_terms, coefs)


def response_sums(moments, ax):
    zero, one = jnp.zeros_like(ax), jnp.ones_like(ax)
    in_terms = jnp.stack(
        [
            jnp.stack([one, zero, zero]),
            jnp.stack([zero, one, zero]),
            jnp.stack([ax, zero, zero]),
            jnp.stack([ax * ax - 2.0 / 3.0, zero, one]),
        ]
    )
    pairs = jnp.sum(in_terms[:, :, None, None, :] * in_terms[None, None, :, :, :], axis=-1)
    spreaded = moments[:, :, None, None, :, :]
    weights = pairs.transpose(0, 2, 3, 1)
    summed = jnp.sum(spreaded * weights, axis=(-1, -2))
    return summed.transpose(0, 2, 1, 3).reshape(moments.shape[0], 4, 12)


def local(observed_heights, ref_map, coefs, shifts, pair_offset, pair_width):
    rows, cols = ref_map.shape
    stride = lax.axis_size("axial")
    tiles = lax.axis_size("azim") * stride
    me = lax.axis_index(AXES)
    row_total = observed_heights.shape[2]
    pair_count = pair_offset.shape[2]
    pair = (me * rows // (row_total // pair_count)).reshape(1)

    words = jnp.concatenate(
        [
            coefs[0, 0],
            shifts[0],
            pair_offset[0, 0].astype(jnp.float32),
            pair_width[0, 0].astype(jnp.float32),
        ]
    )
    words = jnp.pad(words, (0, LANE - words.shape[0]))[None]
    owner = lax.broadcasted_iota(jnp.int32, (tiles, LANE), 0) == me
    table = gather_rows(jnp.where(owner, words, 0.0))
    heights = lax.all_to_all(
        observed_heights[0, 0].reshape(tiles, rows, cols), AXES, 0, 0, tiled=True
    )

    row_place = (me * rows).astype(jnp.float32) + jnp.arange(rows, dtype=jnp.float32)
    ax = (row_place - 0.5 * (row_total - 1)) * (2.0 / row_total)
    row_terms = jnp.broadcast_to(ax[:, None], (rows, LANE))
    col_terms = (jnp.arange(cols, dtype=jnp.float32) - 0.5 * (cols - 1)) * (2.0 / cols)
    col_terms = jnp.broadcast_to(col_terms[None], (8, cols))

    bands, effects, moments = prepare(pair, table, col_terms, stride, pair_count)
    effects = effects[:, :, :3].transpose(2, 0, 1, 3).reshape(3, tiles, cols)
    extra = response_sums(moments[:, :, :3, :3], ax)
    extra = jnp.pad(extra, ((0, 0), (0, 0), (HALF_LANE, LANE - HALF_LANE - 12)))

    map_rows, message = passes(
        pair, table, heights, bands, ref_map, col_terms, row_terms, extra, stride, pair_count
    )
    got = lax.all_to_all(message, AXES, 0, 0, tiled=True)
    new_map, new_coefs = finish(
        me.reshape(1), got, map_rows, effects, row_terms, coefs[0], stride, row_total * cols
    )
    return (new_map, new_coefs[None])


def solution(mesh):
    in_specs = (
        P("axial", "azim", None, None),
        P(("azim", "axial"), None),
        P("axial", "azim", None),
        P("axial", "azim"),
        P("axial", "azim", None),
        P("axial", "azim", None),
    )
    out_specs = (P(("azim", "axial"), None), P("axial", "azim", None))
    return jax.shard_map(local, mesh=mesh, in_specs=in_specs, out_specs=out_specs, check_vma=False)
```

```python
import functools
import math

import jax
import jax.numpy as jnp
from jax import lax
from jax.experimental import pallas as pl
from jax.experimental.pallas import tpu as pltpu
from jax.sharding import PartitionSpec as P

AXES = ("azim", "axial")
WINDOW = 16.0
LANE = 128
WIDE = 256
REACH = 2
BAND = (2 * REACH + 1) * LANE
SPAN = 512
GROUP = 4
HALF_LANE = 64
VMEM_MAIN = 56 * 1024 * 1024
EXACT = lax.Precision.HIGHEST


def exchange(value, axis, steps):
    size = lax.axis_size(axis)
    return sum(lax.ppermute(value, axis, [(i, i ^ k) for i in range(size)]) for k in steps)


def gather_far(value):
    return value + exchange(value, "azim", range(2, lax.axis_size("azim"), 2))


def gather_near(value):
    value = value + exchange(value, "azim", [1])
    step = lax.axis_size("axial") // 2
    while step:
        value = value + exchange(value, "axial", [step])
        step //= 2
    return value


def tap_values(offset):
    centre = offset == 0.0
    angle = jnp.where(centre, 1.0, math.pi * offset)
    sinc = jnp.where(centre, 1.0, jnp.sin(angle) / angle)
    return sinc * jnp.exp(-(offset * offset) / (WINDOW * WINDOW))


def wide_matrix(band_ref, s, way):
    def block(distance):
        if abs(distance) > REACH:
            return jnp.zeros((LANE, LANE), jnp.bfloat16)
        start = (REACH - distance) * LANE
        return band_ref[s, way, :, start : start + LANE]

    rows = []
    for row in range(-2, 4):
        rows.append(jnp.concatenate([block(row - col) for col in range(2)], axis=1))
    return jnp.concatenate(rows, axis=0)


def spread(stacked, rows):
    if rows % 16:
        stacked = stacked.astype(jnp.float32)
    edge = jnp.zeros((rows, WIDE), stacked.dtype)
    before = jnp.concatenate([edge, stacked[:-rows]], axis=0)
    after = jnp.concatenate([stacked[rows:], edge], axis=0)
    return jnp.concatenate([before, stacked, after], axis=1).astype(jnp.bfloat16)


def stack_blocks(value):
    return jnp.concatenate(
        [value[:, k : k + WIDE] for k in range(0, value.shape[1], WIDE)], axis=0
    )


def mixed(stacked, rows, band_ref, s, way):
    return jnp.dot(
        spread(stacked, rows), wide_matrix(band_ref, s, way), preferred_element_type=jnp.float32
    )


def neighbours(s, tiles, stride):
    before = jnp.where(s >= stride, s - stride, s - stride + tiles)
    after = jnp.where(s + stride < tiles, s + stride, s + stride - tiles)
    return before, after


def axis_terms(shape, dim, total, first=0):
    place = lax.broadcasted_iota(jnp.int32, shape, dim).astype(jnp.float32) + first
    return (place - 0.5 * (total - 1)) * (2.0 / total)


def two_parts(value):
    high = value.astype(jnp.bfloat16).astype(jnp.float32)
    return high, value - high


def prepare_kernel(
    tiles, cols, stride, pair_count, pair_ref, words_ref, table_ref,
    band_ref, effect_ref, moment_ref, tap_ref, seen_ref, base_ref
):
    blocks = cols // WIDE
    pair = pair_ref[0]
    place = lax.broadcasted_iota(jnp.int32, (tiles, 2 * SPAN), 1).astype(jnp.float32) - SPAN
    shift = table_ref[:, 4:5]
    tap_ref[0] = tap_values(-place - shift)
    tap_ref[1] = tap_values(place - shift)
    az = axis_terms((8, cols), 1, cols)
    row = lax.broadcasted_iota(jnp.int32, (8, cols), 0)
    base = jnp.where(row == 0, 1.0, jnp.where(row == 1, az, jnp.where(row == 2, az * az, 0.0)))
    high, low = two_parts(base)
    base = jnp.concatenate([high, low], axis=0)
    base_ref[...] = spread(stack_blocks(base).astype(jnp.bfloat16), 16)
    effect_ref[...] = jnp.zeros_like(effect_ref)

    def build(s, carry):
        for way in range(2):
            taps = jnp.broadcast_to(tap_ref[way, pl.ds(s, 1), :], (LANE, 2 * SPAN))
            skewed = pltpu.roll(taps, 0, 1, stride=1, stride_axis=0)
            first = SPAN - REACH * LANE
            band_ref[s, way] = skewed[:, first : first + BAND].astype(jnp.bfloat16)
        out = jnp.dot(
            base_ref[...], wide_matrix(band_ref, s, 0), preferred_element_type=jnp.float32
        )
        seen_ref[s] = jnp.sum(out.reshape(blocks, 2, 8, WIDE), axis=1)
        return carry

    lax.fori_loop(0, tiles, build, 0)
    column = lax.broadcasted_iota(jnp.int32, (2, 8, WIDE), 2) + WIDE * lax.broadcasted_iota(
        jnp.int32, (2, 8, WIDE), 0
    )
    column = column.astype(jnp.float32)
    lanes = lax.broadcasted_iota(jnp.int32, (8, LANE), 1)
    az_blocks = [az[0:1, k : k + LANE] for k in range(0, cols, LANE)]

    def inside(s):
        start = words_ref[s, 5 + pair]
        return (column >= start) & (column < start + words_ref[s, 5 + pair_count + pair])

    def respond(s, carry):
        before, after = neighbours(s, tiles, stride)
        mask_before, mask_own = inside(before), inside(s)
        half = blocks // 2
        own = seen_ref[s]
        zero = jnp.zeros((half, 8, WIDE), jnp.float32)
        parts = [
            jnp.concatenate(
                [jnp.where(mask_before, own[:half], 0.0), jnp.where(mask_own, own[half:], 0.0)], axis=0
            ),
            jnp.concatenate([jnp.where(mask_before, -seen_ref[before][half:], 0.0), zero], axis=0),
            jnp.concatenate([zero, jnp.where(mask_own, -seen_ref[after][:half], 0.0)], axis=0),
        ]
        rows = []
        for block in range(blocks):
            for part in parts:
                rows.extend(two_parts(part[block]))
        out = mixed(jnp.concatenate(rows, axis=0).astype(jnp.bfloat16), 48, band_ref, s, 1)
        out = jnp.sum(out.reshape(blocks, 3, 2, 8, WIDE), axis=2)
        for source, target in enumerate((s, before, after)):
            effect_ref[target] += out[:, source]
            flat = [out[k // 2, source][:, (k % 2) * LANE : (k % 2 + 1) * LANE] for k in range(2 * blocks)]
            first = [f * a for f, a in zip(flat, az_blocks)]
            second = [f * a for f, a in zip(first, az_blocks)]
            sums = [jnp.sum(sum(v), axis=1, keepdims=True) for v in (flat, first, second)]
            moment_ref[s, source] = jnp.where(
                lanes == 0, sums[0], jnp.where(lanes == 1, sums[1], jnp.where(lanes == 2, sums[2], 0.0))
            )
        return carry

    lax.fori_loop(0, tiles, respond, 0)


def prepare(pair, table, cols, stride, pair_count):
    tiles = table.shape[0]
    blocks = cols // WIDE
    vmem = pl.BlockSpec(memory_space=pltpu.VMEM)
    smem = pl.BlockSpec(memory_space=pltpu.SMEM)
    return pl.pallas_call(
        functools.partial(prepare_kernel, tiles, cols, stride, pair_count),
        out_shape=(
            jax.ShapeDtypeStruct((tiles, 2, LANE, BAND), jnp.bfloat16),
            jax.ShapeDtypeStruct((tiles, blocks, 8, WIDE), jnp.float32),
            jax.ShapeDtypeStruct((tiles, 3, 8, LANE), jnp.float32),
        ),
        in_specs=[smem, smem, vmem],
        out_specs=(vmem, vmem, vmem),
        scratch_shapes=[
            pltpu.VMEM((2, tiles, 2 * SPAN), jnp.float32),
            pltpu.VMEM((tiles, blocks, 8, WIDE), jnp.float32),
            pltpu.VMEM((16 * blocks, 3 * WIDE), jnp.bfloat16),
        ],
        compiler_params=pltpu.CompilerParams(vmem_limit_bytes=VMEM_MAIN),
    )(pair, table, table)


def passes_kernel(
    tiles, row_total, stride, pair_count, scale, place_ref, words_ref, height_hbm, band_hbm, ref_ref, extra_ref,
    map_ref, message_ref, height_ref, band_ref, resampled_ref, total_ref, ref_low_ref, sums_ref, sems
):
    rows, cols = ref_ref.shape
    blocks = cols // WIDE
    groups = tiles // GROUP
    pair = place_ref[0]

    def copies(g):
        part = pl.ds(g * GROUP, GROUP)
        return (
            pltpu.make_async_copy(height_hbm.at[part], height_ref.at[part], sems.at[0, g]),
            pltpu.make_async_copy(band_hbm.at[part], band_ref.at[part], sems.at[1, g]),
        )

    for g in range(groups):
        for copy in copies(g):
            copy.start()

    az = axis_terms((1, cols), 1, cols)
    first_row = place_ref[1].astype(jnp.float32)
    ax = axis_terms((rows, LANE), 0, row_total, first_row)
    ax_wide = axis_terms((rows, WIDE), 0, row_total, first_row).reshape(rows // 8, 8, WIDE)
    column = lax.broadcasted_iota(jnp.int32, (2 * rows, WIDE), 1) + jnp.where(
        lax.broadcasted_iota(jnp.int32, (2 * rows, WIDE), 0) >= rows, WIDE, 0
    )
    column = column.astype(jnp.float32)

    def forward(s):
        tilt = ax[:, 0:1]
        shape = (
            words_ref[s, 0]
            + words_ref[s, 1] * az
            + words_ref[s, 2] * tilt
            + words_ref[s, 3] * (az * az + tilt * tilt - 2.0 / 3.0)
        )
        corrected = height_ref[s].astype(jnp.float32) - ref_low_ref[...] - shape
        out = mixed(stack_blocks(corrected).astype(jnp.bfloat16), rows, band_ref, s, 0)
        resampled_ref[s] = out.astype(jnp.bfloat16)

    def seam(left, right):
        difference = resampled_ref[left, 2 * rows :, :].astype(jnp.float32) - resampled_ref[
            right, : 2 * rows, :
        ].astype(jnp.float32)
        start = words_ref[left, 5 + pair]
        inside = (column >= start) & (column < start + words_ref[left, 5 + pair_count + pair])
        return jnp.where(inside, difference, 0.0)

    def backward(s):
        before, after = neighbours(s, tiles, stride)
        upstream = jnp.concatenate([-seam(before, s), seam(s, after)], axis=0).astype(jnp.bfloat16)
        pulled = mixed(upstream, rows, band_ref, s, 1)
        total_ref[...] += pulled
        plain, tilted, bent = [], [], []
        for k in range(blocks):
            block = pulled[k * rows : (k + 1) * rows].reshape(rows // 8, 8, WIDE)
            first = block * ax_wide
            plain.append(jnp.sum(block, axis=0))
            tilted.append(jnp.sum(first, axis=0))
            bent.append(jnp.sum(first * ax_wide, axis=0))
        plain = jnp.concatenate(plain, axis=1)
        tilted = jnp.concatenate(tilted, axis=1)
        bent = jnp.concatenate(bent, axis=1)
        leaning = plain * az
        sums = [plain, leaning, tilted, leaning * az + bent - plain * (2.0 / 3.0)]
        folded = [sum(v[:, k : k + LANE] for k in range(0, cols, LANE)) for v in sums]
        return [jnp.sum(v, axis=0, keepdims=True) for v in folded]

    def add_map(source_ref):
        for k in range(blocks):
            part = slice(k * WIDE, (k + 1) * WIDE)
            map_ref[:, part] = source_ref[:, part] + total_ref[k * rows : (k + 1) * rows, :] / scale

    def first_forward(g, carry):
        for copy in copies(g):
            copy.wait()
        for k in range(GROUP):
            forward(g * GROUP + k)
        return carry

    def first_backward(g, carry):
        for k in range(GROUP):
            s = g * GROUP + k
            for term, value in enumerate(backward(s)):
                sums_ref[term, pl.ds(s, 1), :] = value
        return carry

    ref_low_ref[...] = ref_ref[...].astype(jnp.bfloat16).astype(jnp.float32)
    lax.fori_loop(0, groups, first_forward, 0)
    total_ref[...] = jnp.zeros_like(total_ref)
    lax.fori_loop(0, groups, first_backward, 0)
    add_map(ref_ref)

    ones = jnp.ones((8, LANE), jnp.float32)
    turned = []
    for term in range(4):
        line = lax.dot_general(
            ones, sums_ref[term], (((1,), (1,)), ((), ())),
            precision=EXACT, preferred_element_type=jnp.float32,
        )[0:1]
        if tiles < LANE:
            line = jnp.concatenate([line, jnp.zeros((1, LANE - tiles), jnp.float32)], axis=1)
        turned.append(line)
    turned = jnp.concatenate(turned, axis=0)
    low_lanes = lax.broadcasted_iota(jnp.int32, (4, LANE), 1) < HALF_LANE

    def second_forward(g, carry):
        for k in range(GROUP):
            forward(g * GROUP + k)
        return carry

    def second_backward(g, carry):
        for k in range(GROUP):
            s = g * GROUP + k
            value = jnp.concatenate(backward(s), axis=0)
            value = value + pltpu.roll(value, HALF_LANE, 1)
            value = jnp.where(low_lanes, value, extra_ref[s])
            message_ref[s] = jnp.concatenate([turned, value], axis=0)
        return carry

    ref_low_ref[...] = map_ref[...].astype(jnp.bfloat16).astype(jnp.float32)
    lax.fori_loop(0, groups, second_forward, 0)
    total_ref[...] = jnp.zeros_like(total_ref)
    lax.fori_loop(0, groups, second_backward, 0)
    add_map(map_ref)


def passes(place, table, heights, bands, ref_rows, extra, row_total, stride, pair_count):
    tiles, rows, cols = heights.shape
    vmem = pl.BlockSpec(memory_space=pltpu.VMEM)
    smem = pl.BlockSpec(memory_space=pltpu.SMEM)
    anywhere = pl.BlockSpec(memory_space=pl.ANY)
    return pl.pallas_call(
        functools.partial(passes_kernel, tiles, row_total, stride, pair_count, math.sqrt(tiles)),
        out_shape=(
            jax.ShapeDtypeStruct((rows, cols), jnp.float32),
            jax.ShapeDtypeStruct((tiles, 8, LANE), jnp.float32),
        ),
        in_specs=[smem, smem, anywhere, anywhere, vmem, vmem],
        out_specs=(vmem, vmem),
        scratch_shapes=[
            pltpu.VMEM((tiles, rows, cols), jnp.bfloat16),
            pltpu.VMEM((tiles, 2, LANE, BAND), jnp.bfloat16),
            pltpu.VMEM((tiles, 4 * rows, WIDE), jnp.bfloat16),
            pltpu.VMEM((4 * rows, WIDE), jnp.float32),
            pltpu.VMEM((rows, cols), jnp.float32),
            pltpu.VMEM((4, tiles, LANE), jnp.float32),
            pltpu.SemaphoreType.DMA((2, tiles // GROUP)),
        ],
        compiler_params=pltpu.CompilerParams(vmem_limit_bytes=VMEM_MAIN),
    )(place, table, heights, bands, ref_rows, extra)


def finish_kernel(
    tiles, row_total, stride, scale, pixels, place_ref, got_ref, map_ref, effect_ref, coef_ref, out_map_ref, out_coef_ref
):
    total = jnp.sum(got_ref[...], axis=0)
    step = total[0:4] / pixels
    later = total[4:8]
    lines = lax.broadcasted_iota(jnp.int32, (8, LANE), 0)
    wide = [jnp.broadcast_to(step[k : k + 1], (8, LANE))[:, :tiles] for k in range(4)]
    lines = lines[:, :tiles]
    flat = jnp.where(
        lines == 0, wide[0] - wide[3] * (2.0 / 3.0),
        jnp.where(lines == 1, wide[2], jnp.where(lines == 2, wide[3], 0.0)),
    )
    only = lines == 0

    def weigh(weights, term):
        return jnp.dot(weights, effect_ref[term], precision=EXACT, preferred_element_type=jnp.float32)

    level = weigh(flat, 0)
    level = level + weigh(jnp.where(only, wide[1], 0.0), 1) + weigh(jnp.where(only, wide[3], 0.0), 2)
    ax = axis_terms((map_ref.shape[0], LANE), 0, row_total, place_ref[1].astype(jnp.float32))[:, 0:1]
    change = level[0:1] + ax * (level[1:2] + ax * level[2:3])
    out_map_ref[...] = map_ref[...] - change / scale

    me = place_ref[2]
    before, after = neighbours(me, tiles, stride)
    lane = lax.broadcasted_iota(jnp.int32, (4, LANE), 1)
    reach = jnp.zeros((4, 1), jnp.float32)
    own = None
    for source, target in enumerate((me, before, after)):
        at = jnp.sum(jnp.where(lane == target, step, 0.0), axis=1, keepdims=True)
        own = at if source == 0 else own
        for k in range(4):
            place = HALF_LANE + 4 * source + k
            reach = reach + at[k : k + 1] * later[:, place : place + 1]
    fresh = jnp.sum(jnp.where(lane < HALF_LANE, later, 0.0), axis=1, keepdims=True)
    gain = own + (fresh - reach) / pixels
    line = lax.broadcasted_iota(jnp.int32, (4, LANE), 0)
    gain = jnp.sum(jnp.where(line == lane, gain, 0.0), axis=0, keepdims=True)
    out_coef_ref[...] = coef_ref[...] + gain[:, :4]


def finish(place, got, map_rows, effects, coefs, row_total, stride):
    tiles = got.shape[0]
    vmem = pl.BlockSpec(memory_space=pltpu.VMEM)
    smem = pl.BlockSpec(memory_space=pltpu.SMEM)
    return pl.pallas_call(
        functools.partial(
            finish_kernel, tiles, row_total, stride, math.sqrt(tiles), row_total * map_rows.shape[1]
        ),
        out_shape=(
            jax.ShapeDtypeStruct(map_rows.shape, jnp.float32),
            jax.ShapeDtypeStruct(coefs.shape, jnp.float32),
        ),
        in_specs=[smem] + [vmem] * 4,
        out_specs=(vmem, vmem),
    )(place, got, map_rows, effects, coefs)


def response_sums(moments, ax):
    zero, one = jnp.zeros_like(ax), jnp.ones_like(ax)
    in_terms = jnp.stack(
        [
            jnp.stack([one, zero, zero]),
            jnp.stack([zero, one, zero]),
            jnp.stack([ax, zero, zero]),
            jnp.stack([ax * ax - 2.0 / 3.0, zero, one]),
        ]
    )
    pairs = jnp.sum(in_terms[:, :, None, None, :] * in_terms[None, None, :, :, :], axis=-1)
    spreaded = moments[:, :, None, None, :, :]
    weights = pairs.transpose(0, 2, 3, 1)
    summed = jnp.sum(spreaded * weights, axis=(-1, -2))
    return summed.transpose(0, 2, 1, 3).reshape(moments.shape[0], 4, 12)


def local(observed_heights, ref_map, coefs, shifts, pair_offset, pair_width):
    rows, cols = ref_map.shape
    stride = lax.axis_size("axial")
    tiles = lax.axis_size("azim") * stride
    me = lax.axis_index(AXES)
    row_total = observed_heights.shape[2]
    pair_count = pair_offset.shape[2]
    place = jnp.stack([me * rows // (row_total // pair_count), me * rows, me])

    words = jnp.concatenate(
        [
            coefs[0, 0],
            shifts[0],
            pair_offset[0, 0].astype(jnp.float32),
            pair_width[0, 0].astype(jnp.float32),
        ]
    )
    words = jnp.pad(words, (0, LANE - words.shape[0]))[None]
    owner = lax.broadcasted_iota(jnp.int32, (tiles, LANE), 0) == me
    table = gather_far(jnp.where(owner, words, 0.0))
    table, own_heights = lax.optimization_barrier((table, observed_heights))
    heights = lax.all_to_all(
        own_heights[0, 0].reshape(tiles, rows, cols), AXES, 0, 0, tiled=True
    )
    table = gather_near(table)

    ax = axis_terms((rows,), 0, row_total, (me * rows).astype(jnp.float32))
    bands, effects, moments = prepare(place, table, cols, stride, pair_count)
    effects = effects[:, :, :3].transpose(2, 0, 1, 3).reshape(3, tiles, cols)
    extra = response_sums(moments[:, :, :3, :3], ax)
    extra = jnp.pad(extra, ((0, 0), (0, 0), (HALF_LANE, LANE - HALF_LANE - 12)))

    map_rows, message = passes(
        place, table, heights, bands, ref_map, extra, row_total, stride, pair_count
    )
    got = lax.all_to_all(message, AXES, 0, 0, tiled=True)
    new_map, new_coefs = finish(
        place, got, map_rows, effects, coefs[0], row_total, stride
    )
    return (new_map, new_coefs[None])


def solution(mesh):
    in_specs = (
        P("axial", "azim", None, None),
        P(("azim", "axial"), None),
        P("axial", "azim", None),
        P("axial", "azim"),
        P("axial", "azim", None),
        P("axial", "azim", None),
    )
    out_specs = (P(("azim", "axial"), None), P("axial", "azim", None))
    return jax.shard_map(local, mesh=mesh, in_specs=in_specs, out_specs=out_specs, check_vma=False)
```

```python
import functools
import math

import jax
import jax.numpy as jnp
from jax import lax
from jax.experimental import pallas as pl
from jax.experimental.pallas import tpu as pltpu
from jax.sharding import PartitionSpec as P

AXES = ("azim", "axial")
WINDOW = 16.0
LANE = 128
WIDE = 256
REACH = 2
BAND = (2 * REACH + 1) * LANE
SPAN = 512
GROUP = 16
HALF_LANE = 64
VMEM_LARGE = 56 * 1024 * 1024
VMEM_SMALL = 48 * 1024 * 1024
EXACT = lax.Precision.HIGHEST


def exchange(value, axis, steps):
    size = lax.axis_size(axis)
    return sum(lax.ppermute(value, axis, [(i, i ^ k) for i in range(size)]) for k in steps)


def gather_far(value):
    step = 2
    while step < lax.axis_size("azim"):
        value = value + exchange(value, "azim", [step])
        step *= 2
    return value


def gather_near(value):
    value = value + exchange(value, "azim", [1])
    step = lax.axis_size("axial") // 2
    while step:
        value = value + exchange(value, "axial", [step])
        step //= 2
    return value


def tap_values(offset):
    centre = offset == 0.0
    angle = jnp.where(centre, 1.0, math.pi * offset)
    sinc = jnp.where(centre, 1.0, jnp.sin(angle) / angle)
    return sinc * jnp.exp(-(offset * offset) / (WINDOW * WINDOW))


def wide_matrix(band_ref, s, way):
    def block(distance):
        if abs(distance) > REACH:
            return jnp.zeros((LANE, LANE), jnp.bfloat16)
        start = (REACH - distance) * LANE
        return band_ref[s, way, :, start : start + LANE]

    rows = []
    for row in range(-2, 4):
        rows.append(jnp.concatenate([block(row - col) for col in range(2)], axis=1))
    return jnp.concatenate(rows, axis=0)


def spread(stacked, rows):
    if rows % 16:
        stacked = stacked.astype(jnp.float32)
    edge = jnp.zeros((rows, WIDE), stacked.dtype)
    before = jnp.concatenate([edge, stacked[:-rows]], axis=0)
    after = jnp.concatenate([stacked[rows:], edge], axis=0)
    return jnp.concatenate([before, stacked, after], axis=1).astype(jnp.bfloat16)


def stack_blocks(value):
    return jnp.concatenate(
        [value[:, k : k + WIDE] for k in range(0, value.shape[1], WIDE)], axis=0
    )


def mixed(stacked, rows, band_ref, s, way):
    return jnp.dot(
        spread(stacked, rows), wide_matrix(band_ref, s, way), preferred_element_type=jnp.float32
    )


def neighbours(s, tiles, stride):
    before = jnp.where(s >= stride, s - stride, s - stride + tiles)
    after = jnp.where(s + stride < tiles, s + stride, s + stride - tiles)
    return before, after


def small(tiles):
    return tiles <= HALF_LANE


def vmem_params(tiles):
    return pltpu.CompilerParams(vmem_limit_bytes=VMEM_SMALL if small(tiles) else VMEM_LARGE)


def axis_terms(shape, dim, total, first=0):
    place = lax.broadcasted_iota(jnp.int32, shape, dim).astype(jnp.float32) + first
    return (place - 0.5 * (total - 1)) * (2.0 / total)


def two_parts(value):
    high = value.astype(jnp.bfloat16).astype(jnp.float32)
    return high, value - high


def prepare_kernel(
    tiles, cols, stride, pair_count, pair_ref, words_ref, table_ref,
    band_ref, effect_ref, moment_ref, tap_ref, seen_ref, base_ref
):
    blocks = cols // WIDE
    pair = pair_ref[0]
    place = lax.broadcasted_iota(jnp.int32, (tiles, 2 * SPAN), 1).astype(jnp.float32) - SPAN
    shift = table_ref[:, 4:5]
    tap_ref[0] = tap_values(-place - shift)
    tap_ref[1] = tap_values(place - shift)
    az = axis_terms((8, cols), 1, cols)
    row = lax.broadcasted_iota(jnp.int32, (8, cols), 0)
    base = jnp.where(row == 0, 1.0, jnp.where(row == 1, az, jnp.where(row == 2, az * az, 0.0)))
    high, low = two_parts(base)
    base = jnp.concatenate([high, low], axis=0)
    base_ref[...] = spread(stack_blocks(base).astype(jnp.bfloat16), 16)
    effect_ref[...] = jnp.zeros_like(effect_ref)

    def build(s, carry):
        for way in range(2):
            taps = jnp.broadcast_to(tap_ref[way, pl.ds(s, 1), :], (LANE, 2 * SPAN))
            skewed = pltpu.roll(taps, 0, 1, stride=1, stride_axis=0)
            first = SPAN - REACH * LANE
            band_ref[s, way] = skewed[:, first : first + BAND].astype(jnp.bfloat16)
        out = jnp.dot(
            base_ref[...], wide_matrix(band_ref, s, 0), preferred_element_type=jnp.float32
        )
        seen_ref[s] = jnp.sum(out.reshape(blocks, 2, 8, WIDE), axis=1)
        return carry

    lax.fori_loop(0, tiles, build, 0, unroll=4)
    column = lax.broadcasted_iota(jnp.int32, (2, 8, WIDE), 2) + WIDE * lax.broadcasted_iota(
        jnp.int32, (2, 8, WIDE), 0
    )
    column = column.astype(jnp.float32)
    lanes = lax.broadcasted_iota(jnp.int32, (8, LANE), 1)
    az_blocks = [az[0:1, k : k + LANE] for k in range(0, cols, LANE)]

    def inside(s):
        start = words_ref[s, 5 + pair]
        return (column >= start) & (column < start + words_ref[s, 5 + pair_count + pair])

    def respond(s, carry):
        before, after = neighbours(s, tiles, stride)
        mask_before, mask_own = inside(before), inside(s)
        half = blocks // 2
        own = seen_ref[s]
        zero = jnp.zeros((half, 8, WIDE), jnp.float32)
        parts = [
            jnp.concatenate(
                [jnp.where(mask_before, own[:half], 0.0), jnp.where(mask_own, own[half:], 0.0)], axis=0
            ),
            jnp.concatenate([jnp.where(mask_before, -seen_ref[before][half:], 0.0), zero], axis=0),
            jnp.concatenate([zero, jnp.where(mask_own, -seen_ref[after][:half], 0.0)], axis=0),
        ]
        rows = []
        for block in range(blocks):
            for part in parts:
                rows.extend(two_parts(part[block]))
        out = mixed(jnp.concatenate(rows, axis=0).astype(jnp.bfloat16), 48, band_ref, s, 1)
        out = jnp.sum(out.reshape(blocks, 3, 2, 8, WIDE), axis=2)
        for source, target in enumerate((s, before, after)):
            effect_ref[target] += out[:, source]
            flat = [out[k // 2, source][:, (k % 2) * LANE : (k % 2 + 1) * LANE] for k in range(2 * blocks)]
            first = [f * a for f, a in zip(flat, az_blocks)]
            second = [f * a for f, a in zip(first, az_blocks)]
            sums = [jnp.sum(sum(v), axis=1, keepdims=True) for v in (flat, first, second)]
            moment_ref[s, source] = jnp.where(
                lanes == 0, sums[0], jnp.where(lanes == 1, sums[1], jnp.where(lanes == 2, sums[2], 0.0))
            )
        return carry

    lax.fori_loop(0, tiles, respond, 0, unroll=4)


def prepare(pair, table, cols, stride, pair_count):
    tiles = table.shape[0]
    blocks = cols // WIDE
    vmem = pl.BlockSpec(memory_space=pltpu.VMEM)
    smem = pl.BlockSpec(memory_space=pltpu.SMEM)
    return pl.pallas_call(
        functools.partial(prepare_kernel, tiles, cols, stride, pair_count),
        out_shape=(
            jax.ShapeDtypeStruct((tiles, 2, LANE, BAND), jnp.bfloat16),
            jax.ShapeDtypeStruct((tiles, blocks, 8, WIDE), jnp.float32),
            jax.ShapeDtypeStruct((tiles, 3, 8, LANE), jnp.float32),
        ),
        in_specs=[smem, smem, vmem],
        out_specs=(vmem, vmem, vmem),
        scratch_shapes=[
            pltpu.VMEM((2, tiles, 2 * SPAN), jnp.float32),
            pltpu.VMEM((tiles, blocks, 8, WIDE), jnp.float32),
            pltpu.VMEM((16 * blocks, 3 * WIDE), jnp.bfloat16),
        ],
        compiler_params=vmem_params(tiles),
    )(pair, table, table)


def band_copies(band_hbm, band_ref, sems, g, way):
    part = pl.ds(g * GROUP, GROUP)
    return pltpu.make_async_copy(band_hbm.at[part, way], band_ref.at[part, way], sems.at[way, g])


def one_pass(
    tiles, stride, pair_count, scale, first_row, pair, row_total,
    words_ref, height_ref, band_hbm, ref_ref, map_ref, band_ref, resampled_ref, total_ref, ref_low_ref, sems, keep
):
    rows, cols = ref_ref.shape
    blocks = cols // WIDE
    groups = tiles // GROUP
    for way in range(2):
        for g in range(groups):
            band_copies(band_hbm, band_ref, sems, g, way).start()

    az = axis_terms((1, cols), 1, cols)
    ax = axis_terms((rows, LANE), 0, row_total, first_row)
    ax_wide = axis_terms((rows, WIDE), 0, row_total, first_row).reshape(rows // 8, 8, WIDE)
    column = lax.broadcasted_iota(jnp.int32, (2 * rows, WIDE), 1) + jnp.where(
        lax.broadcasted_iota(jnp.int32, (2 * rows, WIDE), 0) >= rows, WIDE, 0
    )
    column = column.astype(jnp.float32)

    def forward(s):
        tilt = ax[:, 0:1]
        shape = (
            words_ref[s, 0]
            + words_ref[s, 1] * az
            + words_ref[s, 2] * tilt
            + words_ref[s, 3] * (az * az + tilt * tilt - 2.0 / 3.0)
        )
        corrected = height_ref[s].astype(jnp.float32) - ref_low_ref[...] - shape
        out = mixed(stack_blocks(corrected).astype(jnp.bfloat16), rows, band_ref, s, 0)
        resampled_ref[s] = out.astype(jnp.bfloat16)

    def seam(left, right):
        difference = resampled_ref[left, 2 * rows :, :].astype(jnp.float32) - resampled_ref[
            right, : 2 * rows, :
        ].astype(jnp.float32)
        start = words_ref[left, 5 + pair]
        inside = (column >= start) & (column < start + words_ref[left, 5 + pair_count + pair])
        return jnp.where(inside, difference, 0.0)

    def backward(s):
        before, after = neighbours(s, tiles, stride)
        upstream = jnp.concatenate([-seam(before, s), seam(s, after)], axis=0).astype(jnp.bfloat16)
        return mixed(upstream, rows, band_ref, s, 1)

    def term_sums(pulled):
        plain, tilted, bent = [], [], []
        for k in range(blocks):
            block = pulled[k * rows : (k + 1) * rows].reshape(rows // 8, 8, WIDE)
            first = block * ax_wide
            plain.append(jnp.sum(block, axis=0))
            tilted.append(jnp.sum(first, axis=0))
            bent.append(jnp.sum(first * ax_wide, axis=0))
        plain = jnp.concatenate(plain, axis=1)
        tilted = jnp.concatenate(tilted, axis=1)
        bent = jnp.concatenate(bent, axis=1)
        leaning = plain * az
        sums = [plain, leaning, tilted, leaning * az + bent - plain * (2.0 / 3.0)]
        folded = [sum(v[:, k : k + LANE] for k in range(0, cols, LANE)) for v in sums]
        return [jnp.sum(v, axis=0, keepdims=True) for v in folded]

    def all_forward(g, carry):
        band_copies(band_hbm, band_ref, sems, g, 0).wait()
        for k in range(GROUP):
            forward(g * GROUP + k)
        return carry

    def all_backward(g, carry):
        band_copies(band_hbm, band_ref, sems, g, 1).wait()
        for k in range(GROUP):
            s = g * GROUP + k
            pulled = backward(s)
            total_ref[...] += pulled
            if keep is not None:
                for term, value in enumerate(term_sums(pulled)):
                    keep[term, pl.ds(s, 1), :] = value
        return carry

    ref_low_ref[...] = ref_ref[...].astype(jnp.bfloat16).astype(jnp.float32)
    lax.fori_loop(0, groups, all_forward, 0)
    total_ref[...] = jnp.zeros_like(total_ref)
    lax.fori_loop(0, groups, all_backward, 0)
    for k in range(blocks):
        part = slice(k * WIDE, (k + 1) * WIDE)
        map_ref[:, part] = ref_ref[:, part] + total_ref[k * rows : (k + 1) * rows, :] / scale
    return ax_wide


def first_kernel(
    tiles, row_total, stride, pair_count, scale,
    place_ref, words_ref, height_ref, band_hbm, ref_ref, effect_ref, extra_ref, map_ref, message_ref,
    band_ref, resampled_ref, total_ref, ref_low_ref, sums_ref, sems
):
    rows, cols = ref_ref.shape
    ax_wide = one_pass(
        tiles, stride, pair_count, scale, place_ref[1].astype(jnp.float32), place_ref[0], row_total,
        words_ref, height_ref, band_hbm, ref_ref, map_ref, band_ref, resampled_ref, total_ref, ref_low_ref, sems, sums_ref
    )

    def lanes_dot(left, right):
        return lax.dot_general(
            left, right, (((1,), (1,)), ((), ())), precision=EXACT, preferred_element_type=jnp.float32
        )

    ones = jnp.ones((8, LANE), jnp.float32)
    now = jnp.concatenate([lanes_dot(ones, sums_ref[term])[0:1] for term in range(4)], axis=0)

    moments = [[], [], []]
    for k in range(cols // WIDE):
        block = total_ref[k * rows : (k + 1) * rows, :].reshape(rows // 8, 8, WIDE)
        for power in range(3):
            moments[power].append(jnp.sum(jnp.sum(block, axis=0), axis=0, keepdims=True))
            block = block * ax_wide
    moments = [jnp.concatenate(m, axis=1) for m in moments]
    moments = jnp.concatenate(moments + [jnp.zeros((5, cols), jnp.float32)], axis=0)
    level, lean, bend = [lanes_dot(moments, effect_ref[term]) for term in range(3)]
    change = jnp.concatenate(
        [level[0:1], lean[0:1], level[1:2], bend[0:1] + level[2:3] - level[0:1] * (2.0 / 3.0)], axis=0
    )
    later = now - change / scale
    if small(tiles):
        gap = jnp.zeros((4, HALF_LANE - tiles), jnp.float32)
        shared = jnp.concatenate([now, gap, later, gap], axis=1)
    else:
        shared = jnp.concatenate([now, later], axis=0)
    for s in range(tiles):
        message_ref[s] = jnp.concatenate([shared, extra_ref[s]], axis=0)


def second_kernel(
    tiles, row_total, stride, pair_count, scale,
    place_ref, words_ref, height_ref, band_hbm, ref_ref, map_ref,
    band_ref, resampled_ref, total_ref, ref_low_ref, sems
):
    one_pass(
        tiles, stride, pair_count, scale, place_ref[1].astype(jnp.float32), place_ref[0], row_total,
        words_ref, height_ref, band_hbm, ref_ref, map_ref, band_ref, resampled_ref, total_ref, ref_low_ref, sems, None
    )


def in_vmem(value, tiles):
    return pltpu.with_memory_space_constraint(value, pltpu.VMEM) if small(tiles) else value


def run_pass(place, table, heights, bands, ref_rows, more, row_total, stride, pair_count):
    tiles, rows, cols = heights.shape
    vmem = pl.BlockSpec(memory_space=pltpu.VMEM)
    smem = pl.BlockSpec(memory_space=pltpu.SMEM)
    anywhere = pl.BlockSpec(memory_space=pltpu.HBM)
    out_shape = [jax.ShapeDtypeStruct((rows, cols), jnp.float32)]
    scratch = [
        pltpu.VMEM((tiles, 2, LANE, BAND), jnp.bfloat16),
        pltpu.VMEM((tiles, 4 * rows, WIDE), jnp.bfloat16),
        pltpu.VMEM((4 * rows, WIDE), jnp.float32),
        pltpu.VMEM((rows, cols), jnp.float32),
    ]
    if more:
        lines = 8 if small(tiles) else 12
        out_shape.append(jax.ShapeDtypeStruct((tiles, lines, LANE), jnp.float32))
        scratch.append(pltpu.VMEM((4, tiles, LANE), jnp.float32))
    scratch.append(pltpu.SemaphoreType.DMA((2, tiles // GROUP)))
    body = first_kernel if more else second_kernel
    return pl.pallas_call(
        functools.partial(body, tiles, row_total, stride, pair_count, math.sqrt(tiles)),
        out_shape=out_shape,
        in_specs=[smem, smem, vmem, anywhere, vmem] + [vmem] * len(more),
        out_specs=[vmem] * len(out_shape),
        scratch_shapes=scratch,
        compiler_params=vmem_params(tiles),
    )(place, table, heights, bands, ref_rows, *more)


def finish_kernel(
    tiles, row_total, stride, scale, pixels, place_ref, got_ref, map_ref, effect_ref, coef_ref, out_map_ref, out_coef_ref
):
    total = jnp.sum(got_ref[...], axis=0)
    step = total[0:4] / pixels
    if small(tiles):
        later = pltpu.roll(total[0:4], HALF_LANE, 1)
        links = total[4:8]
    else:
        later = total[4:8]
        links = total[8:12]
    lines = lax.broadcasted_iota(jnp.int32, (8, LANE), 0)
    wide = [jnp.broadcast_to(step[k : k + 1], (8, LANE))[:, :tiles] for k in range(4)]
    lines = lines[:, :tiles]
    flat = jnp.where(
        lines == 0, wide[0] - wide[3] * (2.0 / 3.0),
        jnp.where(lines == 1, wide[2], jnp.where(lines == 2, wide[3], 0.0)),
    )
    only = lines == 0

    def weigh(weights, term):
        return jnp.dot(weights, effect_ref[term], precision=EXACT, preferred_element_type=jnp.float32)

    level = weigh(flat, 0)
    level = level + weigh(jnp.where(only, wide[1], 0.0), 1) + weigh(jnp.where(only, wide[3], 0.0), 2)
    ax = axis_terms((map_ref.shape[0], LANE), 0, row_total, place_ref[1].astype(jnp.float32))[:, 0:1]
    change = level[0:1] + ax * (level[1:2] + ax * level[2:3])
    out_map_ref[...] = map_ref[...] - change / scale

    me = place_ref[2]
    before, after = neighbours(me, tiles, stride)
    lane = lax.broadcasted_iota(jnp.int32, (4, LANE), 1)

    def pick(value, target):
        return jnp.sum(jnp.where(lane == target, value, 0.0), axis=1, keepdims=True)

    reach = jnp.zeros((4, 1), jnp.float32)
    for source, target in enumerate((me, before, after)):
        at = pick(step, target)
        for k in range(4):
            place = 4 * source + k
            reach = reach + at[k : k + 1] * links[:, place : place + 1]
    gain = pick(step, me) + (pick(later, me) - reach) / pixels
    line = lax.broadcasted_iota(jnp.int32, (4, LANE), 0)
    gain = jnp.sum(jnp.where(line == lane, gain, 0.0), axis=0, keepdims=True)
    out_coef_ref[...] = coef_ref[...] + gain[:, :4]


def finish(place, got, map_rows, effects, coefs, row_total, stride):
    tiles = got.shape[0]
    vmem = pl.BlockSpec(memory_space=pltpu.VMEM)
    smem = pl.BlockSpec(memory_space=pltpu.SMEM)
    return pl.pallas_call(
        functools.partial(
            finish_kernel, tiles, row_total, stride, math.sqrt(tiles), row_total * map_rows.shape[1]
        ),
        out_shape=(
            jax.ShapeDtypeStruct(map_rows.shape, jnp.float32),
            jax.ShapeDtypeStruct(coefs.shape, jnp.float32),
        ),
        in_specs=[smem] + [vmem] * 4,
        out_specs=(vmem, vmem),
        compiler_params=vmem_params(tiles),
    )(place, got, map_rows, effects, coefs)


def response_sums(moments, ax):
    zero, one = jnp.zeros_like(ax), jnp.ones_like(ax)
    in_terms = jnp.stack(
        [
            jnp.stack([one, zero, zero]),
            jnp.stack([zero, one, zero]),
            jnp.stack([ax, zero, zero]),
            jnp.stack([ax * ax - 2.0 / 3.0, zero, one]),
        ]
    )
    pairs = jnp.sum(in_terms[:, :, None, None, :] * in_terms[None, None, :, :, :], axis=-1)
    spreaded = moments[:, :, None, None, :, :]
    weights = pairs.transpose(0, 2, 3, 1)
    summed = jnp.sum(spreaded * weights, axis=(-1, -2))
    return summed.transpose(0, 2, 1, 3).reshape(moments.shape[0], 4, 12)


def local(observed_heights, ref_map, coefs, shifts, pair_offset, pair_width):
    rows, cols = ref_map.shape
    stride = lax.axis_size("axial")
    tiles = lax.axis_size("azim") * stride
    me = lax.axis_index(AXES)
    row_total = observed_heights.shape[2]
    pair_count = pair_offset.shape[2]
    place = jnp.stack([me * rows // (row_total // pair_count), me * rows, me])

    words = jnp.concatenate(
        [
            coefs[0, 0],
            shifts[0],
            pair_offset[0, 0].astype(jnp.float32),
            pair_width[0, 0].astype(jnp.float32),
        ]
    )
    words = jnp.pad(words, (0, LANE - words.shape[0]))[None]
    owner = lax.broadcasted_iota(jnp.int32, (tiles, LANE), 0) == me
    table = gather_far(jnp.where(owner, words, 0.0))
    table, own_heights = lax.optimization_barrier((table, observed_heights))
    heights = lax.all_to_all(
        own_heights[0, 0].reshape(tiles, rows, cols), AXES, 0, 0, tiled=True
    )
    table = gather_near(table)

    ax = axis_terms((rows,), 0, row_total, (me * rows).astype(jnp.float32))
    bands, effects, moments = prepare(place, table, cols, stride, pair_count)
    effects = effects[:, :, :3].transpose(2, 0, 1, 3).reshape(3, tiles, cols)
    extra = response_sums(moments[:, :, :3, :3], ax)
    extra = jnp.pad(extra, ((0, 0), (0, 0), (0, LANE - 12)))

    heights = in_vmem(heights, tiles)
    map_rows, message = run_pass(
        place, table, heights, bands, ref_map, (effects, extra), row_total, stride, pair_count
    )
    got = in_vmem(lax.all_to_all(message, AXES, 0, 0, tiled=True), tiles)
    (map_rows,) = run_pass(place, table, heights, bands, map_rows, (), row_total, stride, pair_count)
    new_map, new_coefs = finish(place, got, map_rows, effects, coefs[0], row_total, stride)
    return (new_map, new_coefs[None])


def solution(mesh):
    in_specs = (
        P("axial", "azim", None, None),
        P(("azim", "axial"), None),
        P("axial", "azim", None),
        P("axial", "azim"),
        P("axial", "azim", None),
        P("axial", "azim", None),
    )
    out_specs = (P(("azim", "axial"), None), P("axial", "azim", None))
    return jax.shard_map(local, mesh=mesh, in_specs=in_specs, out_specs=out_specs, check_vma=False)
```

```python
import functools
import math

import jax
import jax.numpy as jnp
from jax import lax
from jax.experimental import pallas as pl
from jax.experimental.pallas import tpu as pltpu
from jax.sharding import PartitionSpec as P

AXES = ("azim", "axial")
WINDOW = 16.0
LANE = 128
WIDE = 256
REACH = 2
BAND = 2 * REACH * LANE
SPAN = 256
GROUP = 16
HALF_LANE = 64
VMEM_LARGE = 56 * 1024 * 1024
VMEM_SMALL = 48 * 1024 * 1024
EXACT = lax.Precision.HIGHEST


def exchange(value, axis, steps):
    size = lax.axis_size(axis)
    return sum(lax.ppermute(value, axis, [(i, i ^ k) for i in range(size)]) for k in steps)


def gather_far(value):
    return value + exchange(value, "azim", [lax.axis_size("azim") // 2])


def gather_near(value):
    for axis in ("axial", "azim"):
        step = 1
        while step < lax.axis_size(axis):
            if axis == "axial" or step != lax.axis_size("azim") // 2:
                value = value + exchange(value, axis, [step])
            step *= 2
    return value


def tap_values(lag, shift):
    offset = lag.astype(jnp.float32) - shift
    centre = offset == 0.0
    swing = jnp.sin(math.pi * shift) / math.pi
    swing = jnp.where((lag & 1) == 1, swing, -swing)
    sinc = jnp.where(centre, 1.0, swing / jnp.where(centre, 1.0, offset))
    return sinc * jnp.exp(-(offset * offset) / (WINDOW * WINDOW))


def band_of(taps):
    skewed = pltpu.roll(jnp.broadcast_to(taps, (LANE, BAND)), 0, 1, stride=1, stride_axis=0)
    return skewed.astype(jnp.bfloat16)


def corner_masks():
    row = lax.broadcasted_iota(jnp.int32, (LANE, LANE), 0)
    lane = lax.broadcasted_iota(jnp.int32, (LANE, LANE), 1)
    return [jnp.where(v, 1.0, 0.0).astype(jnp.bfloat16) for v in (lane > row, lane < row)]


def wide_matrix(band, mask_ref):
    def block(distance):
        if abs(distance) > REACH:
            return jnp.zeros((LANE, LANE), jnp.bfloat16)
        if abs(distance) == REACH:
            return band[:, :LANE] * mask_ref[0 if distance > 0 else 1]
        start = (REACH - distance) * LANE
        return band[:, start : start + LANE]

    rows = []
    for row in range(-2, 4):
        rows.append(jnp.concatenate([block(row - col) for col in range(2)], axis=1))
    return jnp.concatenate(rows, axis=0)


def spread(stacked, rows):
    if rows % 16:
        stacked = stacked.astype(jnp.float32)
    edge = jnp.zeros((rows, WIDE), stacked.dtype)
    before = jnp.concatenate([edge, stacked[:-rows]], axis=0)
    after = jnp.concatenate([stacked[rows:], edge], axis=0)
    return jnp.concatenate([before, stacked, after], axis=1).astype(jnp.bfloat16)


def stack_blocks(value):
    return jnp.concatenate(
        [value[:, k : k + WIDE] for k in range(0, value.shape[1], WIDE)], axis=0
    )


def mixed(stacked, rows, band, mask_ref):
    return jnp.dot(
        spread(stacked, rows), wide_matrix(band, mask_ref), preferred_element_type=jnp.float32
    )


def neighbours(s, tiles, stride):
    before = jnp.where(s >= stride, s - stride, s - stride + tiles)
    after = jnp.where(s + stride < tiles, s + stride, s + stride - tiles)
    return before, after


def small(tiles):
    return tiles <= HALF_LANE


def vmem_params(tiles):
    return pltpu.CompilerParams(vmem_limit_bytes=VMEM_SMALL if small(tiles) else VMEM_LARGE)


def axis_terms(shape, dim, total, first=0):
    place = lax.broadcasted_iota(jnp.int32, shape, dim).astype(jnp.float32) + first
    return (place - 0.5 * (total - 1)) * (2.0 / total)


def two_parts(value):
    high = value.astype(jnp.bfloat16).astype(jnp.float32)
    return high, value - high


def prepare_kernel(
    tiles, cols, stride, pair_count, pair_ref, words_ref, table_ref,
    band_ref, effect_ref, moment_ref, tap_ref, back_ref, seen_ref, base_ref, mask_ref
):
    blocks = cols // WIDE
    pair = pair_ref[0]
    place = lax.broadcasted_iota(jnp.int32, (tiles, 2 * SPAN), 1) - SPAN
    shift = table_ref[:, 4:5]
    tap_ref[...] = tap_values(-place, shift)
    back_ref[...] = tap_values(place, shift)
    az = axis_terms((8, cols), 1, cols)
    row = lax.broadcasted_iota(jnp.int32, (8, cols), 0)
    base = jnp.where(row == 0, 1.0, jnp.where(row == 1, az, jnp.where(row == 2, az * az, 0.0)))
    high, low = two_parts(base)
    base = jnp.concatenate([high, low], axis=0)
    base_ref[...] = spread(stack_blocks(base).astype(jnp.bfloat16), 16)
    effect_ref[...] = jnp.zeros_like(effect_ref)
    mask_ref[0], mask_ref[1] = corner_masks()

    def build(s, carry):
        band = band_of(tap_ref[pl.ds(s, 1), :])
        band_ref[0, s] = band
        band_ref[1, s] = band_of(back_ref[pl.ds(s, 1), :])
        out = jnp.dot(base_ref[...], wide_matrix(band, mask_ref), preferred_element_type=jnp.float32)
        seen_ref[s] = jnp.sum(out.reshape(blocks, 2, 8, WIDE), axis=1)
        return carry

    lax.fori_loop(0, tiles, build, 0, unroll=8)
    column = lax.broadcasted_iota(jnp.int32, (2, 8, WIDE), 2) + WIDE * lax.broadcasted_iota(
        jnp.int32, (2, 8, WIDE), 0
    )
    column = column.astype(jnp.float32)
    lanes = lax.broadcasted_iota(jnp.int32, (8, LANE), 1)
    az_blocks = [az[0:1, k : k + LANE] for k in range(0, cols, LANE)]

    def inside(s):
        start = words_ref[s, 5 + pair]
        return (column >= start) & (column < start + words_ref[s, 5 + pair_count + pair])

    def respond(s, carry):
        before, after = neighbours(s, tiles, stride)
        mask_before, mask_own = inside(before), inside(s)
        half = blocks // 2
        own = seen_ref[s]
        zero = jnp.zeros((half, 8, WIDE), jnp.float32)
        parts = [
            jnp.concatenate(
                [jnp.where(mask_before, own[:half], 0.0), jnp.where(mask_own, own[half:], 0.0)], axis=0
            ),
            jnp.concatenate([jnp.where(mask_before, -seen_ref[before][half:], 0.0), zero], axis=0),
            jnp.concatenate([zero, jnp.where(mask_own, -seen_ref[after][:half], 0.0)], axis=0),
        ]
        rows = []
        for block in range(blocks):
            for part in parts:
                rows.extend(two_parts(part[block]))
        stacked = jnp.concatenate(rows, axis=0).astype(jnp.bfloat16)
        out = mixed(stacked, 48, band_ref[1, s], mask_ref)
        out = jnp.sum(out.reshape(blocks, 3, 2, 8, WIDE), axis=2)
        for source, target in enumerate((s, before, after)):
            effect_ref[target] += out[:, source]
            flat = [out[k // 2, source][:, (k % 2) * LANE : (k % 2 + 1) * LANE] for k in range(2 * blocks)]
            first = [f * a for f, a in zip(flat, az_blocks)]
            second = [f * a for f, a in zip(first, az_blocks)]
            sums = [jnp.sum(sum(v), axis=1, keepdims=True) for v in (flat, first, second)]
            moment_ref[s, source] = jnp.where(
                lanes == 0, sums[0], jnp.where(lanes == 1, sums[1], jnp.where(lanes == 2, sums[2], 0.0))
            )
        return carry

    lax.fori_loop(0, tiles, respond, 0, unroll=8)


def prepare(pair, table, cols, stride, pair_count):
    tiles = table.shape[0]
    blocks = cols // WIDE
    vmem = pl.BlockSpec(memory_space=pltpu.VMEM)
    smem = pl.BlockSpec(memory_space=pltpu.SMEM)
    return pl.pallas_call(
        functools.partial(prepare_kernel, tiles, cols, stride, pair_count),
        out_shape=(
            jax.ShapeDtypeStruct((2, tiles, LANE, BAND), jnp.bfloat16),
            jax.ShapeDtypeStruct((tiles, blocks, 8, WIDE), jnp.float32),
            jax.ShapeDtypeStruct((tiles, 3, 8, LANE), jnp.float32),
        ),
        in_specs=[smem, smem, vmem],
        out_specs=(vmem, vmem, vmem),
        scratch_shapes=[
            pltpu.VMEM((tiles, 2 * SPAN), jnp.float32),
            pltpu.VMEM((tiles, 2 * SPAN), jnp.float32),
            pltpu.VMEM((tiles, blocks, 8, WIDE), jnp.float32),
            pltpu.VMEM((16 * blocks, 3 * WIDE), jnp.bfloat16),
            pltpu.VMEM((2, LANE, LANE), jnp.bfloat16),
        ],
        compiler_params=vmem_params(tiles),
    )(pair, table, table)


def band_copy(band_hbm, band_ref, sems, way, g):
    part = pl.ds(g * GROUP, GROUP)
    return pltpu.make_async_copy(band_hbm.at[way, part], band_ref.at[way, part], sems.at[way, g])


def one_pass(
    tiles, stride, pair_count, scale, first_row, pair, row_total,
    words_ref, height_ref, band_hbm, ref_ref, map_ref, band_ref, resampled_ref, total_ref, ref_low_ref, mask_ref, sems, keep
):
    rows, cols = ref_ref.shape
    blocks = cols // WIDE
    groups = tiles // GROUP
    for way in range(2):
        for g in range(groups):
            band_copy(band_hbm, band_ref, sems, way, g).start()

    mask_ref[0], mask_ref[1] = corner_masks()
    az = axis_terms((1, cols), 1, cols)
    ax = axis_terms((rows, LANE), 0, row_total, first_row)[:, 0:1]
    ax_wide = axis_terms((rows, WIDE), 0, row_total, first_row).reshape(rows // 8, 8, WIDE)
    column = lax.broadcasted_iota(jnp.int32, (1, WIDE), 1).astype(jnp.float32)

    def forward(s):
        steep = words_ref[s, 3]
        across = words_ref[s, 0] - steep * (2.0 / 3.0) + az * (words_ref[s, 1] + steep * az)
        along = ax * (words_ref[s, 2] + steep * ax)
        corrected = height_ref[s].astype(jnp.float32) - ref_low_ref[...] - across - along
        out = mixed(stack_blocks(corrected).astype(jnp.bfloat16), rows, band_ref[0, s], mask_ref)
        resampled_ref[s] = out.astype(jnp.bfloat16)

    def backward(s):
        before, after = neighbours(s, tiles, stride)
        half = 2 * rows
        upstream = []
        for owner, other, mine in ((before, before, 0), (s, after, half)):
            low = words_ref[owner, 5 + pair]
            high = low + words_ref[owner, 5 + pair_count + pair]
            theirs = half - mine
            difference = resampled_ref[s, mine : mine + half, :] - resampled_ref[other, theirs : theirs + half, :]
            for block in range(2):
                place = column + block * WIDE
                inside = jnp.where((place >= low) & (place < high), 1.0, 0.0).astype(jnp.bfloat16)
                upstream.append(difference[block * rows : (block + 1) * rows] * inside)
        return mixed(jnp.concatenate(upstream, axis=0), rows, band_ref[1, s], mask_ref)

    def term_sums(pulled):
        plain, tilted, bent = [], [], []
        for k in range(blocks):
            block = pulled[k * rows : (k + 1) * rows].reshape(rows // 8, 8, WIDE)
            first = block * ax_wide
            plain.append(jnp.sum(block, axis=0))
            tilted.append(jnp.sum(first, axis=0))
            bent.append(jnp.sum(first * ax_wide, axis=0))
        plain = jnp.concatenate(plain, axis=1)
        tilted = jnp.concatenate(tilted, axis=1)
        bent = jnp.concatenate(bent, axis=1)
        leaning = plain * az
        sums = [plain, leaning, tilted, leaning * az + bent - plain * (2.0 / 3.0)]
        folded = [sum(v[:, k : k + LANE] for k in range(0, cols, LANE)) for v in sums]
        return [jnp.sum(v, axis=0, keepdims=True) for v in folded]

    def all_forward(g, carry):
        band_copy(band_hbm, band_ref, sems, 0, g).wait()
        for k in range(GROUP):
            forward(g * GROUP + k)
        return carry

    def all_backward(g, carry):
        band_copy(band_hbm, band_ref, sems, 1, g).wait()
        for k in range(GROUP):
            s = g * GROUP + k
            pulled = backward(s)
            total_ref[...] += pulled
            if keep is not None:
                for term, value in enumerate(term_sums(pulled)):
                    keep[term, pl.ds(s, 1), :] = value
        return carry

    ref_low_ref[...] = ref_ref[...].astype(jnp.bfloat16).astype(jnp.float32)
    lax.fori_loop(0, groups, all_forward, 0)
    total_ref[...] = jnp.zeros_like(total_ref)
    lax.fori_loop(0, groups, all_backward, 0)
    for k in range(blocks):
        part = slice(k * WIDE, (k + 1) * WIDE)
        map_ref[:, part] = ref_ref[:, part] + total_ref[k * rows : (k + 1) * rows, :] / scale
    return ax_wide


def first_kernel(
    tiles, row_total, stride, pair_count, scale,
    place_ref, words_ref, height_ref, band_hbm, ref_ref, effect_ref, extra_ref, map_ref, message_ref,
    band_ref, resampled_ref, total_ref, ref_low_ref, mask_ref, sums_ref, sems
):
    rows, cols = ref_ref.shape
    ax_wide = one_pass(
        tiles, stride, pair_count, scale, place_ref[1].astype(jnp.float32), place_ref[0], row_total,
        words_ref, height_ref, band_hbm, ref_ref, map_ref, band_ref, resampled_ref, total_ref, ref_low_ref, mask_ref, sems, sums_ref
    )

    def lanes_dot(left, right):
        return lax.dot_general(
            left, right, (((1,), (1,)), ((), ())), precision=EXACT, preferred_element_type=jnp.float32
        )

    ones = jnp.ones((8, LANE), jnp.float32)
    now = jnp.concatenate([lanes_dot(ones, sums_ref[term])[0:1] for term in range(4)], axis=0)

    moments = [[], [], []]
    for k in range(cols // WIDE):
        block = total_ref[k * rows : (k + 1) * rows, :].reshape(rows // 8, 8, WIDE)
        for power in range(3):
            moments[power].append(jnp.sum(jnp.sum(block, axis=0), axis=0, keepdims=True))
            block = block * ax_wide
    moments = [jnp.concatenate(m, axis=1) for m in moments]
    moments = jnp.concatenate(moments + [jnp.zeros((5, cols), jnp.float32)], axis=0)
    level, lean, bend = [lanes_dot(moments, effect_ref[term]) for term in range(3)]
    change = jnp.concatenate(
        [level[0:1], lean[0:1], level[1:2], bend[0:1] + level[2:3] - level[0:1] * (2.0 / 3.0)], axis=0
    )
    later = now - change / scale
    if small(tiles):
        gap = jnp.zeros((4, HALF_LANE - tiles), jnp.float32)
        shared = jnp.concatenate([now, gap, later, gap], axis=1)
    else:
        shared = jnp.concatenate([now, later], axis=0)
    for s in range(tiles):
        message_ref[s] = jnp.concatenate([shared, extra_ref[s]], axis=0)


def second_kernel(
    tiles, row_total, stride, pair_count, scale,
    place_ref, words_ref, height_ref, band_hbm, ref_ref, map_ref,
    band_ref, resampled_ref, total_ref, ref_low_ref, mask_ref, sems
):
    one_pass(
        tiles, stride, pair_count, scale, place_ref[1].astype(jnp.float32), place_ref[0], row_total,
        words_ref, height_ref, band_hbm, ref_ref, map_ref, band_ref, resampled_ref, total_ref, ref_low_ref, mask_ref, sems, None
    )


def in_vmem(value, tiles):
    return pltpu.with_memory_space_constraint(value, pltpu.VMEM) if small(tiles) else value


def run_pass(place, table, heights, bands, ref_rows, more, row_total, stride, pair_count):
    tiles, rows, cols = heights.shape
    vmem = pl.BlockSpec(memory_space=pltpu.VMEM)
    smem = pl.BlockSpec(memory_space=pltpu.SMEM)
    anywhere = pl.BlockSpec(memory_space=pltpu.HBM)
    out_shape = [jax.ShapeDtypeStruct((rows, cols), jnp.float32)]
    scratch = [
        pltpu.VMEM((2, tiles, LANE, BAND), jnp.bfloat16),
        pltpu.VMEM((tiles, 4 * rows, WIDE), jnp.bfloat16),
        pltpu.VMEM((4 * rows, WIDE), jnp.float32),
        pltpu.VMEM((rows, cols), jnp.float32),
        pltpu.VMEM((2, LANE, LANE), jnp.bfloat16),
    ]
    if more:
        lines = 8 if small(tiles) else 12
        out_shape.append(jax.ShapeDtypeStruct((tiles, lines, LANE), jnp.float32))
        scratch.append(pltpu.VMEM((4, tiles, LANE), jnp.float32))
    scratch.append(pltpu.SemaphoreType.DMA((2, tiles // GROUP)))
    body = first_kernel if more else second_kernel
    return pl.pallas_call(
        functools.partial(body, tiles, row_total, stride, pair_count, math.sqrt(tiles)),
        out_shape=out_shape,
        in_specs=[smem, smem, vmem, anywhere, vmem] + [vmem] * len(more),
        out_specs=[vmem] * len(out_shape),
        scratch_shapes=scratch,
        compiler_params=vmem_params(tiles),
    )(place, table, heights, bands, ref_rows, *more)


def finish_kernel(
    tiles, row_total, stride, scale, pixels, place_ref, got_ref, map_ref, effect_ref, coef_ref, out_map_ref, out_coef_ref
):
    total = jnp.sum(got_ref[...], axis=0)
    step = total[0:4] / pixels
    if small(tiles):
        later = pltpu.roll(total[0:4], HALF_LANE, 1)
        links = total[4:8]
    else:
        later = total[4:8]
        links = total[8:12]
    lines = lax.broadcasted_iota(jnp.int32, (8, LANE), 0)
    wide = [jnp.broadcast_to(step[k : k + 1], (8, LANE))[:, :tiles] for k in range(4)]
    lines = lines[:, :tiles]
    flat = jnp.where(
        lines == 0, wide[0] - wide[3] * (2.0 / 3.0),
        jnp.where(lines == 1, wide[2], jnp.where(lines == 2, wide[3], 0.0)),
    )
    only = lines == 0

    def weigh(weights, term):
        return jnp.dot(weights, effect_ref[term], precision=EXACT, preferred_element_type=jnp.float32)

    level = weigh(flat, 0)
    level = level + weigh(jnp.where(only, wide[1], 0.0), 1) + weigh(jnp.where(only, wide[3], 0.0), 2)
    ax = axis_terms((map_ref.shape[0], LANE), 0, row_total, place_ref[1].astype(jnp.float32))[:, 0:1]
    change = level[0:1] + ax * (level[1:2] + ax * level[2:3])
    out_map_ref[...] = map_ref[...] - change / scale

    me = place_ref[2]
    before, after = neighbours(me, tiles, stride)
    lane = lax.broadcasted_iota(jnp.int32, (4, LANE), 1)

    def pick(value, target):
        return jnp.sum(jnp.where(lane == target, value, 0.0), axis=1, keepdims=True)

    reach = jnp.zeros((4, 1), jnp.float32)
    for source, target in enumerate((me, before, after)):
        at = pick(step, target)
        for k in range(4):
            place = 4 * source + k
            reach = reach + at[k : k + 1] * links[:, place : place + 1]
    gain = pick(step, me) + (pick(later, me) - reach) / pixels
    line = lax.broadcasted_iota(jnp.int32, (4, LANE), 0)
    gain = jnp.sum(jnp.where(line == lane, gain, 0.0), axis=0, keepdims=True)
    out_coef_ref[...] = coef_ref[...] + gain[:, :4]


def finish(place, got, map_rows, effects, coefs, row_total, stride):
    tiles = got.shape[0]
    vmem = pl.BlockSpec(memory_space=pltpu.VMEM)
    smem = pl.BlockSpec(memory_space=pltpu.SMEM)
    return pl.pallas_call(
        functools.partial(
            finish_kernel, tiles, row_total, stride, math.sqrt(tiles), row_total * map_rows.shape[1]
        ),
        out_shape=(
            jax.ShapeDtypeStruct(map_rows.shape, jnp.float32),
            jax.ShapeDtypeStruct(coefs.shape, jnp.float32),
        ),
        in_specs=[smem] + [vmem] * 4,
        out_specs=(vmem, vmem),
        compiler_params=vmem_params(tiles),
    )(place, got, map_rows, effects, coefs)


def response_sums(moments, ax):
    zero, one = jnp.zeros_like(ax), jnp.ones_like(ax)
    in_terms = jnp.stack(
        [
            jnp.stack([one, zero, zero]),
            jnp.stack([zero, one, zero]),
            jnp.stack([ax, zero, zero]),
            jnp.stack([ax * ax - 2.0 / 3.0, zero, one]),
        ]
    )
    pairs = jnp.sum(in_terms[:, :, None, None, :] * in_terms[None, None, :, :, :], axis=-1)
    spreaded = moments[:, :, None, None, :, :]
    weights = pairs.transpose(0, 2, 3, 1)
    summed = jnp.sum(spreaded * weights, axis=(-1, -2))
    return summed.transpose(0, 2, 1, 3).reshape(moments.shape[0], 4, 12)


def local(observed_heights, ref_map, coefs, shifts, pair_offset, pair_width):
    rows, cols = ref_map.shape
    stride = lax.axis_size("axial")
    tiles = lax.axis_size("azim") * stride
    me = lax.axis_index(AXES)
    row_total = observed_heights.shape[2]
    pair_count = pair_offset.shape[2]
    place = jnp.stack([me * rows // (row_total // pair_count), me * rows, me])

    words = jnp.concatenate(
        [
            coefs[0, 0],
            shifts[0],
            pair_offset[0, 0].astype(jnp.float32),
            pair_width[0, 0].astype(jnp.float32),
        ]
    )
    words = jnp.pad(words, (0, LANE - words.shape[0]))[None]
    owner = lax.broadcasted_iota(jnp.int32, (tiles, LANE), 0) == me
    table = gather_far(jnp.where(owner, words, 0.0))
    table, own_heights = lax.optimization_barrier((table, observed_heights))
    heights = lax.all_to_all(
        own_heights[0, 0].reshape(tiles, rows, cols), AXES, 0, 0, tiled=True
    )
    table = gather_near(table)

    ax = axis_terms((rows,), 0, row_total, (me * rows).astype(jnp.float32))
    bands, effects, moments = prepare(place, table, cols, stride, pair_count)
    effects = effects[:, :, :3].transpose(2, 0, 1, 3).reshape(3, tiles, cols)
    extra = response_sums(moments[:, :, :3, :3], ax)
    extra = jnp.pad(extra, ((0, 0), (0, 0), (0, LANE - 12)))

    heights = in_vmem(heights, tiles)
    map_rows, message = run_pass(
        place, table, heights, bands, ref_map, (effects, extra), row_total, stride, pair_count
    )
    got = in_vmem(lax.all_to_all(message, AXES, 0, 0, tiled=True), tiles)
    (map_rows,) = run_pass(
        place, table, heights, bands, map_rows, (), row_total, stride, pair_count
    )
    new_map, new_coefs = finish(place, got, map_rows, effects, coefs[0], row_total, stride)
    return (new_map, new_coefs[None])


def solution(mesh):
    in_specs = (
        P("axial", "azim", None, None),
        P(("azim", "axial"), None),
        P("axial", "azim", None),
        P("axial", "azim"),
        P("axial", "azim", None),
        P("axial", "azim", None),
    )
    out_specs = (P(("azim", "axial"), None), P("axial", "azim", None))
    return jax.shard_map(local, mesh=mesh, in_specs=in_specs, out_specs=out_specs, check_vma=False)
```

```python
import functools
import math

import jax
import jax.numpy as jnp
from jax import lax
from jax.experimental import pallas as pl
from jax.experimental.pallas import tpu as pltpu
from jax.sharding import PartitionSpec as P

AXES = ("azim", "axial")
WINDOW = 16.0
LANE = 128
WIDE = 256
REACH = 2
BAND = 2 * REACH * LANE
SPAN = 256
GROUP = 16
HALF_LANE = 64
VMEM_LARGE = 56 * 1024 * 1024
VMEM_SMALL = 48 * 1024 * 1024
EXACT = lax.Precision.HIGHEST


def exchange(value, axis, steps):
    size = lax.axis_size(axis)
    return sum(lax.ppermute(value, axis, [(i, i ^ k) for i in range(size)]) for k in steps)


def gather_near(value):
    for axis in ("axial", "azim"):
        step = 1
        while step < lax.axis_size(axis):
            if axis == "axial" or step != lax.axis_size("azim") // 2:
                value = value + exchange(value, axis, [step])
            step *= 2
    return value


def tap_values(lag, shift):
    offset = lag.astype(jnp.float32) - shift
    centre = offset == 0.0
    swing = jnp.sin(math.pi * shift) / math.pi
    swing = jnp.where((lag & 1) == 1, swing, -swing)
    sinc = jnp.where(centre, 1.0, swing / jnp.where(centre, 1.0, offset))
    return sinc * jnp.exp(-(offset * offset) / (WINDOW * WINDOW))


def band_of(taps):
    skewed = pltpu.roll(jnp.broadcast_to(taps, (LANE, BAND)), 0, 1, stride=1, stride_axis=0)
    return skewed.astype(jnp.bfloat16)


def corner_masks():
    row = lax.broadcasted_iota(jnp.int32, (LANE, LANE), 0)
    lane = lax.broadcasted_iota(jnp.int32, (LANE, LANE), 1)
    return [jnp.where(v, 1.0, 0.0).astype(jnp.bfloat16) for v in (lane > row, lane < row)]


def wide_matrix(band, mask_ref):
    def block(distance):
        if abs(distance) > REACH:
            return jnp.zeros((LANE, LANE), jnp.bfloat16)
        if abs(distance) == REACH:
            return band[:, :LANE] * mask_ref[0 if distance > 0 else 1]
        start = (REACH - distance) * LANE
        return band[:, start : start + LANE]

    rows = []
    for row in range(-2, 4):
        rows.append(jnp.concatenate([block(row - col) for col in range(2)], axis=1))
    return jnp.concatenate(rows, axis=0)


def spread(stacked, rows):
    if rows % 16:
        stacked = stacked.astype(jnp.float32)
    edge = jnp.zeros((rows, WIDE), stacked.dtype)
    before = jnp.concatenate([edge, stacked[:-rows]], axis=0)
    after = jnp.concatenate([stacked[rows:], edge], axis=0)
    return jnp.concatenate([before, stacked, after], axis=1).astype(jnp.bfloat16)


def stack_blocks(value):
    return jnp.concatenate(
        [value[:, k : k + WIDE] for k in range(0, value.shape[1], WIDE)], axis=0
    )


def mixed(stacked, rows, band, mask_ref):
    return jnp.dot(
        spread(stacked, rows), wide_matrix(band, mask_ref), preferred_element_type=jnp.float32
    )


def neighbours(s, tiles, stride):
    before = jnp.where(s >= stride, s - stride, s - stride + tiles)
    after = jnp.where(s + stride < tiles, s + stride, s + stride - tiles)
    return before, after


def small(tiles):
    return tiles <= HALF_LANE


def vmem_params(tiles):
    return pltpu.CompilerParams(vmem_limit_bytes=VMEM_SMALL if small(tiles) else VMEM_LARGE)


def axis_terms(shape, dim, total, first=0):
    place = lax.broadcasted_iota(jnp.int32, shape, dim).astype(jnp.float32) + first
    return (place - 0.5 * (total - 1)) * (2.0 / total)


def two_parts(value):
    high = value.astype(jnp.bfloat16).astype(jnp.float32)
    return high, value - high


def prepare_kernel(
    tiles, cols, stride, pair_count, pair_ref, words_ref, table_ref,
    band_ref, effect_ref, moment_ref, tap_ref, back_ref, seen_ref, base_ref, mask_ref
):
    blocks = cols // WIDE
    pair = pair_ref[0]
    place = lax.broadcasted_iota(jnp.int32, (tiles, 2 * SPAN), 1) - SPAN
    shift = table_ref[:, 4:5]
    tap_ref[...] = tap_values(-place, shift)
    back_ref[...] = tap_values(place, shift)
    az = axis_terms((8, cols), 1, cols)
    row = lax.broadcasted_iota(jnp.int32, (8, cols), 0)
    base = jnp.where(row == 0, 1.0, jnp.where(row == 1, az, jnp.where(row == 2, az * az, 0.0)))
    high, low = two_parts(base)
    base = jnp.concatenate([high, low], axis=0)
    base_ref[...] = spread(stack_blocks(base).astype(jnp.bfloat16), 16)
    effect_ref[...] = jnp.zeros_like(effect_ref)
    mask_ref[0], mask_ref[1] = corner_masks()

    def build(s, carry):
        band = band_of(tap_ref[pl.ds(s, 1), :])
        band_ref[0, s] = band
        band_ref[1, s] = band_of(back_ref[pl.ds(s, 1), :])
        out = jnp.dot(base_ref[...], wide_matrix(band, mask_ref), preferred_element_type=jnp.float32)
        seen_ref[s] = jnp.sum(out.reshape(blocks, 2, 8, WIDE), axis=1)
        return carry

    lax.fori_loop(0, tiles, build, 0, unroll=16)
    column = lax.broadcasted_iota(jnp.int32, (2, 8, WIDE), 2) + WIDE * lax.broadcasted_iota(
        jnp.int32, (2, 8, WIDE), 0
    )
    column = column.astype(jnp.float32)
    lanes = lax.broadcasted_iota(jnp.int32, (8, LANE), 1)
    az_blocks = [az[0:1, k : k + LANE] for k in range(0, cols, LANE)]

    def inside(s):
        start = words_ref[s, 5 + pair]
        return (column >= start) & (column < start + words_ref[s, 5 + pair_count + pair])

    def respond(s, carry):
        before, after = neighbours(s, tiles, stride)
        mask_before, mask_own = inside(before), inside(s)
        half = blocks // 2
        own = seen_ref[s]
        zero = jnp.zeros((half, 8, WIDE), jnp.float32)
        parts = [
            jnp.concatenate(
                [jnp.where(mask_before, own[:half], 0.0), jnp.where(mask_own, own[half:], 0.0)], axis=0
            ),
            jnp.concatenate([jnp.where(mask_before, -seen_ref[before][half:], 0.0), zero], axis=0),
            jnp.concatenate([zero, jnp.where(mask_own, -seen_ref[after][:half], 0.0)], axis=0),
        ]
        rows = []
        for block in range(blocks):
            for part in parts:
                rows.extend(two_parts(part[block]))
        stacked = jnp.concatenate(rows, axis=0).astype(jnp.bfloat16)
        out = mixed(stacked, 48, band_ref[1, s], mask_ref)
        out = jnp.sum(out.reshape(blocks, 3, 2, 8, WIDE), axis=2)
        for source, target in enumerate((s, before, after)):
            effect_ref[target] += out[:, source]
            flat = [out[k // 2, source][:, (k % 2) * LANE : (k % 2 + 1) * LANE] for k in range(2 * blocks)]
            first = [f * a for f, a in zip(flat, az_blocks)]
            second = [f * a for f, a in zip(first, az_blocks)]
            sums = [jnp.sum(sum(v), axis=1, keepdims=True) for v in (flat, first, second)]
            moment_ref[s, source] = jnp.where(
                lanes == 0, sums[0], jnp.where(lanes == 1, sums[1], jnp.where(lanes == 2, sums[2], 0.0))
            )
        return carry

    lax.fori_loop(0, tiles, respond, 0, unroll=16)


def prepare(pair, table, cols, stride, pair_count):
    tiles = table.shape[0]
    blocks = cols // WIDE
    vmem = pl.BlockSpec(memory_space=pltpu.VMEM)
    smem = pl.BlockSpec(memory_space=pltpu.SMEM)
    return pl.pallas_call(
        functools.partial(prepare_kernel, tiles, cols, stride, pair_count),
        out_shape=(
            jax.ShapeDtypeStruct((2, tiles, LANE, BAND), jnp.bfloat16),
            jax.ShapeDtypeStruct((tiles, blocks, 8, WIDE), jnp.float32),
            jax.ShapeDtypeStruct((tiles, 3, 8, LANE), jnp.float32),
        ),
        in_specs=[smem, smem, vmem],
        out_specs=(vmem, vmem, vmem),
        scratch_shapes=[
            pltpu.VMEM((tiles, 2 * SPAN), jnp.float32),
            pltpu.VMEM((tiles, 2 * SPAN), jnp.float32),
            pltpu.VMEM((tiles, blocks, 8, WIDE), jnp.float32),
            pltpu.VMEM((16 * blocks, 3 * WIDE), jnp.bfloat16),
            pltpu.VMEM((2, LANE, LANE), jnp.bfloat16),
        ],
        compiler_params=vmem_params(tiles),
    )(pair, table, table)


def band_copy(band_hbm, band_ref, sems, way, g):
    part = pl.ds(g * GROUP, GROUP)
    return pltpu.make_async_copy(band_hbm.at[way, part], band_ref.at[way, part], sems.at[way, g])


def one_pass(
    tiles, stride, pair_count, scale, first_row, pair, row_total,
    words_ref, height_ref, band_hbm, ref_ref, map_ref, band_ref, resampled_ref, total_ref, ref_low_ref, mask_ref, sems, keep
):
    rows, cols = ref_ref.shape
    blocks = cols // WIDE
    groups = tiles // GROUP
    for way in range(2):
        for g in range(groups):
            band_copy(band_hbm, band_ref, sems, way, g).start()

    mask_ref[0], mask_ref[1] = corner_masks()
    az = axis_terms((1, cols), 1, cols)
    ax = axis_terms((rows, LANE), 0, row_total, first_row)[:, 0:1]
    ax_wide = axis_terms((rows, WIDE), 0, row_total, first_row).reshape(rows // 8, 8, WIDE)
    column = lax.broadcasted_iota(jnp.int32, (1, WIDE), 1).astype(jnp.float32)

    def forward(s):
        steep = words_ref[s, 3]
        across = words_ref[s, 0] - steep * (2.0 / 3.0) + az * (words_ref[s, 1] + steep * az)
        along = ax * (words_ref[s, 2] + steep * ax)
        corrected = height_ref[s].astype(jnp.float32) - ref_low_ref[...] - across - along
        out = mixed(stack_blocks(corrected).astype(jnp.bfloat16), rows, band_ref[0, s], mask_ref)
        resampled_ref[s] = out.astype(jnp.bfloat16)

    def backward(s):
        before, after = neighbours(s, tiles, stride)
        half = 2 * rows
        upstream = []
        for owner, other, mine in ((before, before, 0), (s, after, half)):
            low = words_ref[owner, 5 + pair]
            high = low + words_ref[owner, 5 + pair_count + pair]
            theirs = half - mine
            difference = resampled_ref[s, mine : mine + half, :] - resampled_ref[other, theirs : theirs + half, :]
            for block in range(2):
                place = column + block * WIDE
                inside = jnp.where((place >= low) & (place < high), 1.0, 0.0).astype(jnp.bfloat16)
                upstream.append(difference[block * rows : (block + 1) * rows] * inside)
        return mixed(jnp.concatenate(upstream, axis=0), rows, band_ref[1, s], mask_ref)

    def term_sums(pulled):
        plain, tilted, bent = [], [], []
        for k in range(blocks):
            block = pulled[k * rows : (k + 1) * rows].reshape(rows // 8, 8, WIDE)
            first = block * ax_wide
            plain.append(jnp.sum(block, axis=0))
            tilted.append(jnp.sum(first, axis=0))
            bent.append(jnp.sum(first * ax_wide, axis=0))
        plain = jnp.concatenate(plain, axis=1)
        tilted = jnp.concatenate(tilted, axis=1)
        bent = jnp.concatenate(bent, axis=1)
        leaning = plain * az
        sums = [plain, leaning, tilted, leaning * az + bent - plain * (2.0 / 3.0)]
        folded = [sum(v[:, k : k + LANE] for k in range(0, cols, LANE)) for v in sums]
        return [jnp.sum(v, axis=0, keepdims=True) for v in folded]

    def all_forward(g, carry):
        band_copy(band_hbm, band_ref, sems, 0, g).wait()
        for k in range(GROUP):
            forward(g * GROUP + k)
        return carry

    def all_backward(g, carry):
        band_copy(band_hbm, band_ref, sems, 1, g).wait()
        for k in range(GROUP):
            s = g * GROUP + k
            pulled = backward(s)
            total_ref[...] += pulled
            if keep is not None:
                for term, value in enumerate(term_sums(pulled)):
                    keep[term, pl.ds(s, 1), :] = value
        return carry

    ref_low_ref[...] = ref_ref[...].astype(jnp.bfloat16).astype(jnp.float32)
    lax.fori_loop(0, groups, all_forward, 0)
    total_ref[...] = jnp.zeros_like(total_ref)
    lax.fori_loop(0, groups, all_backward, 0)
    for k in range(blocks):
        part = slice(k * WIDE, (k + 1) * WIDE)
        map_ref[:, part] = ref_ref[:, part] + total_ref[k * rows : (k + 1) * rows, :] / scale
    return ax_wide


def first_kernel(
    tiles, row_total, stride, pair_count, scale,
    place_ref, words_ref, height_ref, band_hbm, ref_ref, effect_ref, extra_ref, map_ref, message_ref,
    band_ref, resampled_ref, total_ref, ref_low_ref, mask_ref, sums_ref, sems
):
    rows, cols = ref_ref.shape
    ax_wide = one_pass(
        tiles, stride, pair_count, scale, place_ref[1].astype(jnp.float32), place_ref[0], row_total,
        words_ref, height_ref, band_hbm, ref_ref, map_ref, band_ref, resampled_ref, total_ref, ref_low_ref, mask_ref, sems, sums_ref
    )

    def lanes_dot(left, right):
        return lax.dot_general(
            left, right, (((1,), (1,)), ((), ())), precision=EXACT, preferred_element_type=jnp.float32
        )

    ones = jnp.ones((8, LANE), jnp.float32)
    now = jnp.concatenate([lanes_dot(ones, sums_ref[term])[0:1] for term in range(4)], axis=0)

    moments = [[], [], []]
    for k in range(cols // WIDE):
        block = total_ref[k * rows : (k + 1) * rows, :].reshape(rows // 8, 8, WIDE)
        for power in range(3):
            moments[power].append(jnp.sum(jnp.sum(block, axis=0), axis=0, keepdims=True))
            block = block * ax_wide
    moments = [jnp.concatenate(m, axis=1) for m in moments]
    moments = jnp.concatenate(moments + [jnp.zeros((5, cols), jnp.float32)], axis=0)
    level, lean, bend = [lanes_dot(moments, effect_ref[term]) for term in range(3)]
    change = jnp.concatenate(
        [level[0:1], lean[0:1], level[1:2], bend[0:1] + level[2:3] - level[0:1] * (2.0 / 3.0)], axis=0
    )
    later = now - change / scale
    if small(tiles):
        gap = jnp.zeros((4, HALF_LANE - tiles), jnp.float32)
        shared = jnp.concatenate([now, gap, later, gap], axis=1)
    else:
        shared = jnp.concatenate([now, later], axis=0)
    for s in range(tiles):
        message_ref[s] = jnp.concatenate([shared, extra_ref[s]], axis=0)


def second_kernel(
    tiles, row_total, stride, pair_count, scale,
    place_ref, words_ref, height_ref, band_hbm, ref_ref, map_ref,
    band_ref, resampled_ref, total_ref, ref_low_ref, mask_ref, sems
):
    one_pass(
        tiles, stride, pair_count, scale, place_ref[1].astype(jnp.float32), place_ref[0], row_total,
        words_ref, height_ref, band_hbm, ref_ref, map_ref, band_ref, resampled_ref, total_ref, ref_low_ref, mask_ref, sems, None
    )


def in_vmem(value, tiles):
    return pltpu.with_memory_space_constraint(value, pltpu.VMEM) if small(tiles) else value


def run_pass(place, table, heights, bands, ref_rows, more, row_total, stride, pair_count):
    tiles, rows, cols = heights.shape
    vmem = pl.BlockSpec(memory_space=pltpu.VMEM)
    smem = pl.BlockSpec(memory_space=pltpu.SMEM)
    anywhere = pl.BlockSpec(memory_space=pltpu.HBM)
    out_shape = [jax.ShapeDtypeStruct((rows, cols), jnp.float32)]
    scratch = [
        pltpu.VMEM((2, tiles, LANE, BAND), jnp.bfloat16),
        pltpu.VMEM((tiles, 4 * rows, WIDE), jnp.bfloat16),
        pltpu.VMEM((4 * rows, WIDE), jnp.float32),
        pltpu.VMEM((rows, cols), jnp.float32),
        pltpu.VMEM((2, LANE, LANE), jnp.bfloat16),
    ]
    if more:
        lines = 8 if small(tiles) else 12
        out_shape.append(jax.ShapeDtypeStruct((tiles, lines, LANE), jnp.float32))
        scratch.append(pltpu.VMEM((4, tiles, LANE), jnp.float32))
    scratch.append(pltpu.SemaphoreType.DMA((2, tiles // GROUP)))
    body = first_kernel if more else second_kernel
    return pl.pallas_call(
        functools.partial(body, tiles, row_total, stride, pair_count, math.sqrt(tiles)),
        out_shape=out_shape,
        in_specs=[smem, smem, vmem, anywhere, vmem] + [vmem] * len(more),
        out_specs=[vmem] * len(out_shape),
        scratch_shapes=scratch,
        compiler_params=vmem_params(tiles),
    )(place, table, heights, bands, ref_rows, *more)


def finish_kernel(
    tiles, row_total, stride, scale, pixels, place_ref, got_ref, map_ref, effect_ref, coef_ref, out_map_ref, out_coef_ref
):
    total = jnp.sum(got_ref[...], axis=0)
    step = total[0:4] / pixels
    if small(tiles):
        later = pltpu.roll(total[0:4], HALF_LANE, 1)
        links = total[4:8]
    else:
        later = total[4:8]
        links = total[8:12]
    lines = lax.broadcasted_iota(jnp.int32, (8, LANE), 0)
    wide = [jnp.broadcast_to(step[k : k + 1], (8, LANE))[:, :tiles] for k in range(4)]
    lines = lines[:, :tiles]
    flat = jnp.where(
        lines == 0, wide[0] - wide[3] * (2.0 / 3.0),
        jnp.where(lines == 1, wide[2], jnp.where(lines == 2, wide[3], 0.0)),
    )
    only = lines == 0

    def weigh(weights, term):
        return jnp.dot(weights, effect_ref[term], precision=EXACT, preferred_element_type=jnp.float32)

    level = weigh(flat, 0)
    level = level + weigh(jnp.where(only, wide[1], 0.0), 1) + weigh(jnp.where(only, wide[3], 0.0), 2)
    ax = axis_terms((map_ref.shape[0], LANE), 0, row_total, place_ref[1].astype(jnp.float32))[:, 0:1]
    change = level[0:1] + ax * (level[1:2] + ax * level[2:3])
    out_map_ref[...] = map_ref[...] - change / scale

    me = place_ref[2]
    before, after = neighbours(me, tiles, stride)
    lane = lax.broadcasted_iota(jnp.int32, (4, LANE), 1)

    def pick(value, target):
        return jnp.sum(jnp.where(lane == target, value, 0.0), axis=1, keepdims=True)

    reach = jnp.zeros((4, 1), jnp.float32)
    for source, target in enumerate((me, before, after)):
        at = pick(step, target)
        for k in range(4):
            place = 4 * source + k
            reach = reach + at[k : k + 1] * links[:, place : place + 1]
    gain = pick(step, me) + (pick(later, me) - reach) / pixels
    line = lax.broadcasted_iota(jnp.int32, (4, LANE), 0)
    gain = jnp.sum(jnp.where(line == lane, gain, 0.0), axis=0, keepdims=True)
    out_coef_ref[...] = coef_ref[...] + gain[:, :4]


def finish(place, got, map_rows, effects, coefs, row_total, stride):
    tiles = got.shape[0]
    vmem = pl.BlockSpec(memory_space=pltpu.VMEM)
    smem = pl.BlockSpec(memory_space=pltpu.SMEM)
    return pl.pallas_call(
        functools.partial(
            finish_kernel, tiles, row_total, stride, math.sqrt(tiles), row_total * map_rows.shape[1]
        ),
        out_shape=(
            jax.ShapeDtypeStruct(map_rows.shape, jnp.float32),
            jax.ShapeDtypeStruct(coefs.shape, jnp.float32),
        ),
        in_specs=[smem] + [vmem] * 4,
        out_specs=(vmem, vmem),
        compiler_params=vmem_params(tiles),
    )(place, got, map_rows, effects, coefs)


def response_sums(moments, ax):
    zero, one = jnp.zeros_like(ax), jnp.ones_like(ax)
    in_terms = jnp.stack(
        [
            jnp.stack([one, zero, zero]),
            jnp.stack([zero, one, zero]),
            jnp.stack([ax, zero, zero]),
            jnp.stack([ax * ax - 2.0 / 3.0, zero, one]),
        ]
    )
    pairs = jnp.sum(in_terms[:, :, None, None, :] * in_terms[None, None, :, :, :], axis=-1)
    spreaded = moments[:, :, None, None, :, :]
    weights = pairs.transpose(0, 2, 3, 1)
    summed = jnp.sum(spreaded * weights, axis=(-1, -2))
    return summed.transpose(0, 2, 1, 3).reshape(moments.shape[0], 4, 12)


def local(observed_heights, ref_map, coefs, shifts, pair_offset, pair_width):
    rows, cols = ref_map.shape
    stride = lax.axis_size("axial")
    tiles = lax.axis_size("azim") * stride
    me = lax.axis_index(AXES)
    row_total = observed_heights.shape[2]
    pair_count = pair_offset.shape[2]
    place = jnp.stack([me * rows // (row_total // pair_count), me * rows, me])

    words = jnp.concatenate(
        [
            coefs[0, 0],
            shifts[0],
            pair_offset[0, 0].astype(jnp.float32),
            pair_width[0, 0].astype(jnp.float32),
        ]
    )
    words = jnp.pad(words, (0, LANE - words.shape[0]))[None]
    far = lax.axis_size("azim") // 2
    theirs = exchange(words, "azim", [far])
    theirs, own_heights = lax.optimization_barrier((theirs, observed_heights))
    line = lax.broadcasted_iota(jnp.int32, (tiles, LANE), 0)
    them = (lax.axis_index("azim") ^ far) * stride + lax.axis_index("axial")
    table = jnp.where(line == me, words, jnp.where(line == them, theirs, 0.0))
    heights = lax.all_to_all(
        own_heights[0, 0].reshape(tiles, rows, cols), AXES, 0, 0, tiled=True
    )
    table = gather_near(table)

    ax = axis_terms((rows,), 0, row_total, (me * rows).astype(jnp.float32))
    bands, effects, moments = prepare(place, table, cols, stride, pair_count)
    effects = effects[:, :, :3].transpose(2, 0, 1, 3).reshape(3, tiles, cols)
    extra = response_sums(moments[:, :, :3, :3], ax)
    extra = jnp.pad(extra, ((0, 0), (0, 0), (0, LANE - 12)))

    heights = in_vmem(heights, tiles)
    map_rows, message = run_pass(
        place, table, heights, bands, ref_map, (effects, extra), row_total, stride, pair_count
    )
    got = in_vmem(lax.all_to_all(message, AXES, 0, 0, tiled=True), tiles)
    (map_rows,) = run_pass(
        place, table, heights, bands, map_rows, (), row_total, stride, pair_count
    )
    new_map, new_coefs = finish(place, got, map_rows, effects, coefs[0], row_total, stride)
    return (new_map, new_coefs[None])


def solution(mesh):
    in_specs = (
        P("axial", "azim", None, None),
        P(("azim", "axial"), None),
        P("axial", "azim", None),
        P("axial", "azim"),
        P("axial", "azim", None),
        P("axial", "azim", None),
    )
    out_specs = (P(("azim", "axial"), None), P("axial", "azim", None))
    return jax.shard_map(local, mesh=mesh, in_specs=in_specs, out_specs=out_specs, check_vma=False)
```

```python
import functools
import math

import jax
import jax.numpy as jnp
from jax import lax
from jax.experimental import pallas as pl
from jax.experimental.pallas import tpu as pltpu
from jax.sharding import PartitionSpec as P

AXES = ("azim", "axial")
WINDOW = 16.0
LANE = 128
WIDE = 256
REACH = 2
BAND = 2 * REACH * LANE
SPAN = 256
GROUP = 16
HALF_LANE = 64
LINK_LANE = 96
VMEM_LARGE = 56 * 1024 * 1024
VMEM_SMALL = 48 * 1024 * 1024
EXACT = lax.Precision.HIGHEST


def exchange(value, axis, steps):
    size = lax.axis_size(axis)
    return sum(lax.ppermute(value, axis, [(i, i ^ k) for i in range(size)]) for k in steps)


def gather_near(value):
    for axis in ("axial", "azim"):
        step = 1
        while step < lax.axis_size(axis):
            if axis == "axial" or step != lax.axis_size("azim") // 2:
                value = value + exchange(value, axis, [step])
            step *= 2
    return value


def tap_values(lag, shift):
    offset = lag.astype(jnp.float32) - shift
    centre = offset == 0.0
    swing = jnp.sin(math.pi * shift) / math.pi
    swing = jnp.where((lag & 1) == 1, swing, -swing)
    sinc = jnp.where(centre, 1.0, swing / jnp.where(centre, 1.0, offset))
    return sinc * jnp.exp(-(offset * offset) / (WINDOW * WINDOW))


def band_of(taps):
    skewed = pltpu.roll(jnp.broadcast_to(taps, (LANE, BAND)), 0, 1, stride=1, stride_axis=0)
    return skewed.astype(jnp.bfloat16)


def corner_masks():
    row = lax.broadcasted_iota(jnp.int32, (LANE, LANE), 0)
    lane = lax.broadcasted_iota(jnp.int32, (LANE, LANE), 1)
    return [jnp.where(v, 1.0, 0.0).astype(jnp.bfloat16) for v in (lane > row, lane < row)]


def wide_matrix(band, mask_ref):
    def block(distance):
        if abs(distance) > REACH:
            return jnp.zeros((LANE, LANE), jnp.bfloat16)
        if abs(distance) == REACH:
            return band[:, :LANE] * mask_ref[0 if distance > 0 else 1]
        start = (REACH - distance) * LANE
        return band[:, start : start + LANE]

    rows = []
    for row in range(-2, 4):
        rows.append(jnp.concatenate([block(row - col) for col in range(2)], axis=1))
    return jnp.concatenate(rows, axis=0)


def spread(stacked, rows):
    if rows % 16:
        stacked = stacked.astype(jnp.float32)
    edge = jnp.zeros((rows, WIDE), stacked.dtype)
    before = jnp.concatenate([edge, stacked[:-rows]], axis=0)
    after = jnp.concatenate([stacked[rows:], edge], axis=0)
    return jnp.concatenate([before, stacked, after], axis=1).astype(jnp.bfloat16)


def stack_blocks(value):
    return jnp.concatenate(
        [value[:, k : k + WIDE] for k in range(0, value.shape[1], WIDE)], axis=0
    )


def mixed(stacked, rows, band, mask_ref):
    return jnp.dot(
        spread(stacked, rows), wide_matrix(band, mask_ref), preferred_element_type=jnp.float32
    )


def neighbours(s, tiles, stride):
    before = jnp.where(s >= stride, s - stride, s - stride + tiles)
    after = jnp.where(s + stride < tiles, s + stride, s + stride - tiles)
    return before, after


def small(tiles):
    return tiles <= LANE - LINK_LANE


def vmem_params(tiles):
    return pltpu.CompilerParams(vmem_limit_bytes=VMEM_SMALL if small(tiles) else VMEM_LARGE)


def axis_terms(shape, dim, total, first=0):
    place = lax.broadcasted_iota(jnp.int32, shape, dim).astype(jnp.float32) + first
    return (place - 0.5 * (total - 1)) * (2.0 / total)


def two_parts(value):
    high = value.astype(jnp.bfloat16).astype(jnp.float32)
    return high, value - high


def prepare_kernel(
    tiles, cols, stride, pair_count, pair_ref, words_ref, table_ref,
    band_ref, effect_ref, moment_ref, tap_ref, back_ref, seen_ref, base_ref, mask_ref
):
    blocks = cols // WIDE
    pair = pair_ref[0]
    place = lax.broadcasted_iota(jnp.int32, (tiles, 2 * SPAN), 1) - SPAN
    shift = table_ref[:, 4:5]
    tap_ref[...] = tap_values(-place, shift)
    back_ref[...] = tap_values(place, shift)
    az = axis_terms((8, cols), 1, cols)
    row = lax.broadcasted_iota(jnp.int32, (8, cols), 0)
    base = jnp.where(row == 0, 1.0, jnp.where(row == 1, az, jnp.where(row == 2, az * az, 0.0)))
    high, low = two_parts(base)
    base = jnp.concatenate([high, low], axis=0)
    base_ref[...] = spread(stack_blocks(base).astype(jnp.bfloat16), 16)
    effect_ref[...] = jnp.zeros_like(effect_ref)
    mask_ref[0], mask_ref[1] = corner_masks()

    def build(s, carry):
        band = band_of(tap_ref[pl.ds(s, 1), :])
        band_ref[0, s] = band
        band_ref[1, s] = band_of(back_ref[pl.ds(s, 1), :])
        out = jnp.dot(base_ref[...], wide_matrix(band, mask_ref), preferred_element_type=jnp.float32)
        seen_ref[s] = jnp.sum(out.reshape(blocks, 2, 8, WIDE), axis=1)
        return carry

    lax.fori_loop(0, tiles, build, 0, unroll=32)
    column = lax.broadcasted_iota(jnp.int32, (2, 8, WIDE), 2) + WIDE * lax.broadcasted_iota(
        jnp.int32, (2, 8, WIDE), 0
    )
    column = column.astype(jnp.float32)
    lanes = lax.broadcasted_iota(jnp.int32, (8, LANE), 1)
    az_blocks = [az[0:1, k : k + LANE] for k in range(0, cols, LANE)]

    def inside(s):
        start = words_ref[s, 5 + pair]
        return (column >= start) & (column < start + words_ref[s, 5 + pair_count + pair])

    def respond(s, carry):
        before, after = neighbours(s, tiles, stride)
        mask_before, mask_own = inside(before), inside(s)
        half = blocks // 2
        own = seen_ref[s]
        zero = jnp.zeros((half, 8, WIDE), jnp.float32)
        parts = [
            jnp.concatenate(
                [jnp.where(mask_before, own[:half], 0.0), jnp.where(mask_own, own[half:], 0.0)], axis=0
            ),
            jnp.concatenate([jnp.where(mask_before, -seen_ref[before][half:], 0.0), zero], axis=0),
            jnp.concatenate([zero, jnp.where(mask_own, -seen_ref[after][:half], 0.0)], axis=0),
        ]
        rows = []
        for block in range(blocks):
            for part in parts:
                rows.extend(two_parts(part[block]))
        stacked = jnp.concatenate(rows, axis=0).astype(jnp.bfloat16)
        out = mixed(stacked, 48, band_ref[1, s], mask_ref)
        out = jnp.sum(out.reshape(blocks, 3, 2, 8, WIDE), axis=2)
        for source, target in enumerate((s, before, after)):
            effect_ref[target] += out[:, source]
            flat = [out[k // 2, source][:, (k % 2) * LANE : (k % 2 + 1) * LANE] for k in range(2 * blocks)]
            first = [f * a for f, a in zip(flat, az_blocks)]
            second = [f * a for f, a in zip(first, az_blocks)]
            sums = [jnp.sum(sum(v), axis=1, keepdims=True) for v in (flat, first, second)]
            moment_ref[s, source] = jnp.where(
                lanes == 0, sums[0], jnp.where(lanes == 1, sums[1], jnp.where(lanes == 2, sums[2], 0.0))
            )
        return carry

    lax.fori_loop(0, tiles, respond, 0, unroll=32)


def prepare(pair, table, cols, stride, pair_count):
    tiles = table.shape[0]
    blocks = cols // WIDE
    vmem = pl.BlockSpec(memory_space=pltpu.VMEM)
    smem = pl.BlockSpec(memory_space=pltpu.SMEM)
    return pl.pallas_call(
        functools.partial(prepare_kernel, tiles, cols, stride, pair_count),
        out_shape=(
            jax.ShapeDtypeStruct((2, tiles, LANE, BAND), jnp.bfloat16),
            jax.ShapeDtypeStruct((tiles, blocks, 8, WIDE), jnp.float32),
            jax.ShapeDtypeStruct((tiles, 3, 8, LANE), jnp.float32),
        ),
        in_specs=[smem, smem, vmem],
        out_specs=(vmem, vmem, vmem),
        scratch_shapes=[
            pltpu.VMEM((tiles, 2 * SPAN), jnp.float32),
            pltpu.VMEM((tiles, 2 * SPAN), jnp.float32),
            pltpu.VMEM((tiles, blocks, 8, WIDE), jnp.float32),
            pltpu.VMEM((16 * blocks, 3 * WIDE), jnp.bfloat16),
            pltpu.VMEM((2, LANE, LANE), jnp.bfloat16),
        ],
        compiler_params=vmem_params(tiles),
    )(pair, table, table)


def band_copy(band_hbm, band_ref, sems, way, g):
    part = pl.ds(g * GROUP, GROUP)
    return pltpu.make_async_copy(band_hbm.at[way, part], band_ref.at[way, part], sems.at[way, g])


def one_pass(
    tiles, stride, pair_count, scale, first_row, pair, row_total,
    words_ref, height_ref, band_hbm, ref_ref, map_ref, band_ref, resampled_ref, total_ref, ref_low_ref, mask_ref, sems, keep
):
    rows, cols = ref_ref.shape
    blocks = cols // WIDE
    groups = tiles // GROUP
    for way in range(2):
        for g in range(groups):
            band_copy(band_hbm, band_ref, sems, way, g).start()

    mask_ref[0], mask_ref[1] = corner_masks()
    az = axis_terms((1, cols), 1, cols)
    ax = axis_terms((rows, LANE), 0, row_total, first_row)[:, 0:1]
    ax_wide = axis_terms((rows, WIDE), 0, row_total, first_row).reshape(rows // 8, 8, WIDE)
    column = lax.broadcasted_iota(jnp.int32, (1, WIDE), 1).astype(jnp.float32)

    def forward(s):
        steep = words_ref[s, 3]
        across = words_ref[s, 0] - steep * (2.0 / 3.0) + az * (words_ref[s, 1] + steep * az)
        along = ax * (words_ref[s, 2] + steep * ax)
        corrected = height_ref[s].astype(jnp.float32) - ref_low_ref[...] - across - along
        out = mixed(stack_blocks(corrected).astype(jnp.bfloat16), rows, band_ref[0, s], mask_ref)
        resampled_ref[s] = out.astype(jnp.bfloat16)

    def backward(s):
        before, after = neighbours(s, tiles, stride)
        half = 2 * rows
        upstream = []
        for owner, other, mine in ((before, before, 0), (s, after, half)):
            low = words_ref[owner, 5 + pair]
            high = low + words_ref[owner, 5 + pair_count + pair]
            theirs = half - mine
            difference = resampled_ref[s, mine : mine + half, :] - resampled_ref[other, theirs : theirs + half, :]
            for block in range(2):
                place = column + block * WIDE
                inside = jnp.where((place >= low) & (place < high), 1.0, 0.0).astype(jnp.bfloat16)
                upstream.append(difference[block * rows : (block + 1) * rows] * inside)
        return mixed(jnp.concatenate(upstream, axis=0), rows, band_ref[1, s], mask_ref)

    def term_sums(pulled):
        plain, tilted, bent = [], [], []
        for k in range(blocks):
            block = pulled[k * rows : (k + 1) * rows].reshape(rows // 8, 8, WIDE)
            first = block * ax_wide
            plain.append(jnp.sum(block, axis=0))
            tilted.append(jnp.sum(first, axis=0))
            bent.append(jnp.sum(first * ax_wide, axis=0))
        plain = jnp.concatenate(plain, axis=1)
        tilted = jnp.concatenate(tilted, axis=1)
        bent = jnp.concatenate(bent, axis=1)
        leaning = plain * az
        sums = [plain, leaning, tilted, leaning * az + bent - plain * (2.0 / 3.0)]
        folded = [sum(v[:, k : k + LANE] for k in range(0, cols, LANE)) for v in sums]
        return [jnp.sum(v, axis=0, keepdims=True) for v in folded]

    def all_forward(g, carry):
        band_copy(band_hbm, band_ref, sems, 0, g).wait()
        for k in range(GROUP):
            forward(g * GROUP + k)
        return carry

    def all_backward(g, carry):
        band_copy(band_hbm, band_ref, sems, 1, g).wait()
        for k in range(GROUP):
            s = g * GROUP + k
            pulled = backward(s)
            total_ref[...] += pulled
            if keep is not None:
                for term, value in enumerate(term_sums(pulled)):
                    keep[term, pl.ds(s, 1), :] = value
        return carry

    ref_low_ref[...] = ref_ref[...].astype(jnp.bfloat16).astype(jnp.float32)
    lax.fori_loop(0, groups, all_forward, 0)
    total_ref[...] = jnp.zeros_like(total_ref)
    lax.fori_loop(0, groups, all_backward, 0)
    for k in range(blocks):
        part = slice(k * WIDE, (k + 1) * WIDE)
        map_ref[:, part] = ref_ref[:, part] + total_ref[k * rows : (k + 1) * rows, :] / scale
    return ax_wide


def first_kernel(
    tiles, row_total, stride, pair_count, scale,
    place_ref, words_ref, height_ref, band_hbm, ref_ref, effect_ref, extra_ref, map_ref, message_ref,
    band_ref, resampled_ref, total_ref, ref_low_ref, mask_ref, sums_ref, sems
):
    rows, cols = ref_ref.shape
    ax_wide = one_pass(
        tiles, stride, pair_count, scale, place_ref[1].astype(jnp.float32), place_ref[0], row_total,
        words_ref, height_ref, band_hbm, ref_ref, map_ref, band_ref, resampled_ref, total_ref, ref_low_ref, mask_ref, sems, sums_ref
    )

    def lanes_dot(left, right):
        return lax.dot_general(
            left, right, (((1,), (1,)), ((), ())), precision=EXACT, preferred_element_type=jnp.float32
        )

    ones = jnp.ones((8, LANE), jnp.float32)
    now = jnp.concatenate([lanes_dot(ones, sums_ref[term])[0:1] for term in range(4)], axis=0)

    moments = [[], [], []]
    for k in range(cols // WIDE):
        block = total_ref[k * rows : (k + 1) * rows, :].reshape(rows // 8, 8, WIDE)
        for power in range(3):
            moments[power].append(jnp.sum(jnp.sum(block, axis=0), axis=0, keepdims=True))
            block = block * ax_wide
    moments = [jnp.concatenate(m, axis=1) for m in moments]
    moments = jnp.concatenate(moments + [jnp.zeros((5, cols), jnp.float32)], axis=0)
    level, lean, bend = [lanes_dot(moments, effect_ref[term]) for term in range(3)]
    change = jnp.concatenate(
        [level[0:1], lean[0:1], level[1:2], bend[0:1] + level[2:3] - level[0:1] * (2.0 / 3.0)], axis=0
    )
    later = now - change / scale
    if small(tiles):
        gap = jnp.zeros((4, HALF_LANE - tiles), jnp.float32)
        shared = jnp.concatenate([now, gap, later, gap], axis=1)
    else:
        shared = jnp.concatenate([now, later], axis=0)
    for s in range(tiles):
        if small(tiles):
            message_ref[s] = shared + extra_ref[s]
        else:
            message_ref[s] = jnp.concatenate([shared, extra_ref[s]], axis=0)


def second_kernel(
    tiles, row_total, stride, pair_count, scale,
    place_ref, words_ref, height_ref, band_hbm, ref_ref, map_ref,
    band_ref, resampled_ref, total_ref, ref_low_ref, mask_ref, sems
):
    one_pass(
        tiles, stride, pair_count, scale, place_ref[1].astype(jnp.float32), place_ref[0], row_total,
        words_ref, height_ref, band_hbm, ref_ref, map_ref, band_ref, resampled_ref, total_ref, ref_low_ref, mask_ref, sems, None
    )


def in_vmem(value, tiles):
    return pltpu.with_memory_space_constraint(value, pltpu.VMEM) if small(tiles) else value


def run_pass(place, table, heights, bands, ref_rows, more, row_total, stride, pair_count):
    tiles, rows, cols = heights.shape
    vmem = pl.BlockSpec(memory_space=pltpu.VMEM)
    smem = pl.BlockSpec(memory_space=pltpu.SMEM)
    anywhere = pl.BlockSpec(memory_space=pltpu.HBM)
    out_shape = [jax.ShapeDtypeStruct((rows, cols), jnp.float32)]
    scratch = [
        pltpu.VMEM((2, tiles, LANE, BAND), jnp.bfloat16),
        pltpu.VMEM((tiles, 4 * rows, WIDE), jnp.bfloat16),
        pltpu.VMEM((4 * rows, WIDE), jnp.float32),
        pltpu.VMEM((rows, cols), jnp.float32),
        pltpu.VMEM((2, LANE, LANE), jnp.bfloat16),
    ]
    if more:
        lines = 4 if small(tiles) else 12
        out_shape.append(jax.ShapeDtypeStruct((tiles, lines, LANE), jnp.float32))
        scratch.append(pltpu.VMEM((4, tiles, LANE), jnp.float32))
    scratch.append(pltpu.SemaphoreType.DMA((2, tiles // GROUP)))
    body = first_kernel if more else second_kernel
    return pl.pallas_call(
        functools.partial(body, tiles, row_total, stride, pair_count, math.sqrt(tiles)),
        out_shape=out_shape,
        in_specs=[smem, smem, vmem, anywhere, vmem] + [vmem] * len(more),
        out_specs=[vmem] * len(out_shape),
        scratch_shapes=scratch,
        compiler_params=vmem_params(tiles),
    )(place, table, heights, bands, ref_rows, *more)


def finish_kernel(
    tiles, row_total, stride, scale, pixels, place_ref, got_ref, map_ref, effect_ref, coef_ref, out_map_ref, out_coef_ref
):
    total = jnp.sum(got_ref[...], axis=0)
    step = total[0:4] / pixels
    if small(tiles):
        later = pltpu.roll(total[0:4], HALF_LANE, 1)
        links = total[0:4]
    else:
        later = total[4:8]
        links = total[8:12]
    lines = lax.broadcasted_iota(jnp.int32, (8, LANE), 0)
    wide = [jnp.broadcast_to(step[k : k + 1], (8, LANE))[:, :tiles] for k in range(4)]
    lines = lines[:, :tiles]
    flat = jnp.where(
        lines == 0, wide[0] - wide[3] * (2.0 / 3.0),
        jnp.where(lines == 1, wide[2], jnp.where(lines == 2, wide[3], 0.0)),
    )
    only = lines == 0

    def weigh(weights, term):
        return jnp.dot(weights, effect_ref[term], precision=EXACT, preferred_element_type=jnp.float32)

    level = weigh(flat, 0)
    level = level + weigh(jnp.where(only, wide[1], 0.0), 1) + weigh(jnp.where(only, wide[3], 0.0), 2)
    ax = axis_terms((map_ref.shape[0], LANE), 0, row_total, place_ref[1].astype(jnp.float32))[:, 0:1]
    change = level[0:1] + ax * (level[1:2] + ax * level[2:3])
    out_map_ref[...] = map_ref[...] - change / scale

    me = place_ref[2]
    before, after = neighbours(me, tiles, stride)
    lane = lax.broadcasted_iota(jnp.int32, (4, LANE), 1)

    def pick(value, target):
        return jnp.sum(jnp.where(lane == target, value, 0.0), axis=1, keepdims=True)

    reach = jnp.zeros((4, 1), jnp.float32)
    for source, target in enumerate((me, before, after)):
        at = pick(step, target)
        for k in range(4):
            place = 4 * source + k + (LINK_LANE if small(tiles) else 0)
            reach = reach + at[k : k + 1] * links[:, place : place + 1]
    gain = pick(step, me) + (pick(later, me) - reach) / pixels
    line = lax.broadcasted_iota(jnp.int32, (4, LANE), 0)
    gain = jnp.sum(jnp.where(line == lane, gain, 0.0), axis=0, keepdims=True)
    out_coef_ref[...] = coef_ref[...] + gain[:, :4]


def finish(place, got, map_rows, effects, coefs, row_total, stride):
    tiles = got.shape[0]
    vmem = pl.BlockSpec(memory_space=pltpu.VMEM)
    smem = pl.BlockSpec(memory_space=pltpu.SMEM)
    return pl.pallas_call(
        functools.partial(
            finish_kernel, tiles, row_total, stride, math.sqrt(tiles), row_total * map_rows.shape[1]
        ),
        out_shape=(
            jax.ShapeDtypeStruct(map_rows.shape, jnp.float32),
            jax.ShapeDtypeStruct(coefs.shape, jnp.float32),
        ),
        in_specs=[smem] + [vmem] * 4,
        out_specs=(vmem, vmem),
        compiler_params=vmem_params(tiles),
    )(place, got, map_rows, effects, coefs)


def response_sums(moments, ax):
    zero, one = jnp.zeros_like(ax), jnp.ones_like(ax)
    in_terms = jnp.stack(
        [
            jnp.stack([one, zero, zero]),
            jnp.stack([zero, one, zero]),
            jnp.stack([ax, zero, zero]),
            jnp.stack([ax * ax - 2.0 / 3.0, zero, one]),
        ]
    )
    pairs = jnp.sum(in_terms[:, :, None, None, :] * in_terms[None, None, :, :, :], axis=-1)
    spreaded = moments[:, :, None, None, :, :]
    weights = pairs.transpose(0, 2, 3, 1)
    summed = jnp.sum(spreaded * weights, axis=(-1, -2))
    return summed.transpose(0, 2, 1, 3).reshape(moments.shape[0], 4, 12)


def local(observed_heights, ref_map, coefs, shifts, pair_offset, pair_width):
    rows, cols = ref_map.shape
    stride = lax.axis_size("axial")
    tiles = lax.axis_size("azim") * stride
    me = lax.axis_index(AXES)
    row_total = observed_heights.shape[2]
    pair_count = pair_offset.shape[2]
    place = jnp.stack([me * rows // (row_total // pair_count), me * rows, me])

    words = jnp.concatenate(
        [
            coefs[0, 0],
            shifts[0],
            pair_offset[0, 0].astype(jnp.float32),
            pair_width[0, 0].astype(jnp.float32),
        ]
    )
    words = jnp.pad(words, (0, LANE - words.shape[0]))[None]
    far = lax.axis_size("azim") // 2
    theirs = exchange(words, "azim", [far])
    theirs, own_heights = lax.optimization_barrier((theirs, observed_heights))
    line = lax.broadcasted_iota(jnp.int32, (tiles, LANE), 0)
    them = (lax.axis_index("azim") ^ far) * stride + lax.axis_index("axial")
    table = jnp.where(line == me, words, jnp.where(line == them, theirs, 0.0))
    heights = lax.all_to_all(
        own_heights[0, 0].reshape(tiles, rows, cols), AXES, 0, 0, tiled=True
    )
    table = gather_near(table)

    ax = axis_terms((rows,), 0, row_total, (me * rows).astype(jnp.float32))
    bands, effects, moments = prepare(place, table, cols, stride, pair_count)
    effects = effects[:, :, :3].transpose(2, 0, 1, 3).reshape(3, tiles, cols)
    extra = response_sums(moments[:, :, :3, :3], ax)
    left = LINK_LANE if small(tiles) else 0
    extra = jnp.pad(extra, ((0, 0), (0, 0), (left, LANE - 12 - left)))

    heights = in_vmem(heights, tiles)
    map_rows, message = run_pass(
        place, table, heights, bands, ref_map, (effects, extra), row_total, stride, pair_count
    )
    got = in_vmem(lax.all_to_all(message, AXES, 0, 0, tiled=True), tiles)
    (map_rows,) = run_pass(
        place, table, heights, bands, map_rows, (), row_total, stride, pair_count
    )
    new_map, new_coefs = finish(place, got, map_rows, effects, coefs[0], row_total, stride)
    return (new_map, new_coefs[None])


def solution(mesh):
    in_specs = (
        P("axial", "azim", None, None),
        P(("azim", "axial"), None),
        P("axial", "azim", None),
        P("axial", "azim"),
        P("axial", "azim", None),
        P("axial", "azim", None),
    )
    out_specs = (P(("azim", "axial"), None), P("axial", "azim", None))
    return jax.shard_map(local, mesh=mesh, in_specs=in_specs, out_specs=out_specs, check_vma=False)
```
